512 devices in a mesh: seg: 16 (over y, x_hi, core), space: 32 (over z, x_lo).
Axes of the slice: x: 4 (x_hi: 2, x_lo: 2; x = x_hi * 2 + x_lo), y: 4, z: 16, core: 2. Of those that a mesh axis runs over, the one named last changes fastest.
Arguments:
- field: float32 [16, 192, 384, 128], P('seg', 'space'), may hold values from -6 to 6
- base: float32 [16, 192, 384, 128], P('seg', 'space'), may hold values from -5 to 5
- radial_step: float32 [192, 192], replicated, may hold values from -1 to 1
- az_shift: int32 [1], replicated, may hold values from 0 to 383
- ax_shift: int32 [1], replicated, may hold values from 0 to 8191
- first_segment: int32 [1], replicated, may hold values from 0 to 1023
Outputs:
- mismatch: float32 [16, 192, 384, 128], P('seg', 'space')
The draws below stay inside these ranges and needn't reach their ends.
All inputs are finite; a program needn't handle non-finite values.
Results may differ from the reference program's by a relative error of at most 0.0001.
Values sent between devices are 32-bit elements; how exact they have to be, the bound alone decides.
No kernel may reach another device: no remote copies, remote signals or barrier semaphores. Data moves between devices by JAX's collectives and lax.ppermute only.
A program may use at most 64 MiB of HBM per device.

```python
import math
import jax
import jax.numpy as jnp
from jax import lax

NR = 192
NT = 384
NZ = 128
STEPS = 2
SEGS = 16


def draw_radial_step(key, part):
    noise = jnp.clip(jax.random.normal(key, (NR, NR), jnp.float32), -4.0, 4.0)
    return 0.7 * jnp.eye(NR, dtype=jnp.float32) + 0.6 / math.sqrt(NR) * noise


def block_levels(rng, dims, pieces, least, high):
    level, own = 1.0, jax.random.fold_in(rng, 6)
    for dim, parts in pieces:
        draws = jnp.exp(jax.random.uniform(jax.random.fold_in(own, dim), (parts,), jnp.float32, least / len(pieces), high / len(pieces)))
        level = level * jnp.repeat(draws, dims[dim] // parts).reshape([-1 if axis == dim else 1 for axis in range(len(dims))])
    return level


def bell_draw(key, shape, deviation, bound, split=(), kind=jnp.bfloat16):
    entries = jax.random.normal(key, shape, jnp.float32) * deviation
    if len(split) > 0:
        entries = block_levels(key, shape, split, -0.22, 0.18) * entries
    return jnp.clip(entries, min=-bound, max=bound).astype(kind)


def setup_inputs(seed: int = 0) -> dict:
    arg_keys = jax.random.split(jax.random.key(seed), 7)
    return {
        "field": bell_draw(arg_keys[0], (SEGS, NR, NT, NZ), 1.0, 6.0, ((0, 16), (1, 32)), jnp.float32),
        "base": bell_draw(arg_keys[1], (SEGS, NR, NT, NZ), 1.0, 5.0, ((0, 16), (1, 32)), jnp.float32),
        "radial_step": draw_radial_step(jax.random.fold_in(arg_keys[6], 71), 0),
        "az_shift": jax.random.randint(arg_keys[3], (1,), 0, NT).astype(jnp.int32),
        "ax_shift": jax.random.randint(arg_keys[4], (1,), 0, 64 * NZ).astype(jnp.int32),
        "first_segment": jax.random.randint(arg_keys[5], (1,), 0, 64 * SEGS).astype(jnp.int32),
    }


step_size = 0.25
viscous_rate = 1.5e-05

def real_fourier(size):
    rows = jnp.arange(size, dtype=jnp.int32)
    wave = jnp.where(rows == 0, 0, jnp.where(rows == 1, size // 2, rows // 2)).astype(jnp.int32)
    phase = wave[:, None] * rows[None, :] % size
    angle = phase.astype(jnp.float32) * jnp.float32(2.0 * math.pi / size)
    sine = (rows % 2 == 1) & (rows >= 3)
    row_scale = jnp.where(rows < 2, jnp.float32(math.sqrt(1.0 / size)), jnp.float32(math.sqrt(2.0 / size)))
    table = row_scale[:, None] * jnp.where(sine[:, None], jnp.sin(angle), jnp.cos(angle))
    return (table.astype(jnp.float32), wave)

def make_tables():
    table_t, wave_t = real_fourier(NT)
    table_z, wave_z = real_fourier(NZ)
    float_t = wave_t.astype(jnp.float32)
    float_z = wave_z.astype(jnp.float32)
    decay = jnp.exp(jnp.float32(-viscous_rate) * (float_t[:, None] * float_t[:, None] + float_z[None, :] * float_z[None, :]))
    return (table_t, table_z, decay.astype(jnp.float32))

def advance(state, base, radial_step, table_t, table_z, decay):
    exact = lax.Precision.HIGHEST
    for repeat in range(STEPS):
        forced = state + step_size * base * state
        spectral = jnp.einsum('mt,rtz->rmz', table_t, forced, precision=exact)
        spectral = jnp.einsum('kz,rmz->rmk', table_z, spectral, precision=exact)
        spectral = spectral * decay[None]
        spectral = jnp.einsum('qr,rmk->qmk', radial_step, spectral, precision=exact)
        state = jnp.einsum('mt,rmk->rtk', table_t, spectral, precision=exact)
        state = jnp.einsum('kz,rtk->rtz', table_z, state, precision=exact)
    return state

def reflect_shift(state, azimuth, axial):
    places_t = jnp.arange(NT, dtype=jnp.int32)
    places_z = jnp.arange(NZ, dtype=jnp.int32)
    index_t = ((azimuth - places_t) % NT).astype(jnp.int32)
    index_z = ((places_z + axial) % NZ).astype(jnp.int32)
    state = jnp.take(state, index_t, axis=1)
    return jnp.take(state, index_z, axis=2)

def reference(field, base, radial_step, az_shift, ax_shift, first_segment):
    table_t, table_z, decay = make_tables()

    def one_segment(pair):
        return advance(pair[0], pair[1], radial_step, table_t, table_z, decay)
    ends = lax.map(one_segment, (field, base))
    carried = jnp.roll(ends, 1, axis=0)
    start = (first_segment[0] % SEGS).astype(jnp.int32)
    picked = lax.dynamic_index_in_dim(carried, start, 0, keepdims=False)
    moved = reflect_shift(picked, az_shift[0], ax_shift[0])
    carried = lax.dynamic_update_index_in_dim(carried, moved, start, 0)
    return carried - field
```

```python
import math

import jax
import jax.numpy as jnp
import numpy as np
from jax import lax
from jax.sharding import PartitionSpec as P

STEP_SIZE = 0.25
VISCOUS_RATE = 1.5e-05
EXACT = lax.Precision.HIGHEST


def filter_table(size):
    rows = np.arange(size)
    wave = np.where(rows == 0, 0, np.where(rows == 1, size // 2, rows // 2))
    angle = (wave[:, None] * rows[None, :] % size) * (2.0 * math.pi / size)
    sine = (rows % 2 == 1) & (rows >= 3)
    scale = np.where(rows < 2, math.sqrt(1.0 / size), math.sqrt(2.0 / size))
    table = scale[:, None] * np.where(sine[:, None], np.sin(angle), np.cos(angle))
    decay = np.exp(-VISCOUS_RATE * wave.astype(np.float64) ** 2)
    return (table.T @ (decay[:, None] * table)).astype(np.float32)


def from_behind(block, axis, distance):
    devices = range(lax.axis_size(axis))
    route = [((i - distance) % len(devices), i) for i in devices]
    return lax.ppermute(block, axis, route)


def to_points(block, parts):
    radii, count_t, count_z = block.shape
    share = count_t // parts
    packed = block.reshape(radii, parts, share, count_z).swapaxes(0, 1)
    packed = packed.reshape(parts, radii * share, count_z)
    packed = lax.all_to_all(packed, "space", 0, 0, tiled=True)
    return packed.reshape(parts * radii, share, count_z)


def to_radii(block, parts):
    count_r, share, count_z = block.shape
    radii = count_r // parts
    packed = block.reshape(parts, radii * share, count_z)
    packed = lax.all_to_all(packed, "space", 0, 0, tiled=True)
    packed = packed.reshape(parts, radii, share, count_z).swapaxes(0, 1)
    return packed.reshape(radii, parts * share, count_z)


def apply_filter(state, table_t, table_z):
    state = jnp.einsum("ts,rsz->rtz", table_t, state, precision=EXACT)
    return jnp.einsum("rtz,zk->rtk", state, table_z, precision=EXACT)


def shards(field, base, radial_step, az_shift, ax_shift, first_segment):
    state = field[0]
    own_base = base[0]
    count_t, count_z = state.shape[1:]
    parts = lax.axis_size("space")
    table_t = jnp.asarray(filter_table(count_t))
    table_z = jnp.asarray(filter_table(count_z))

    with jax.named_scope("first_filter"):
        filtered = apply_filter(state + STEP_SIZE * own_base * state, table_t, table_z)
    with jax.named_scope("shift_state"):
        filtered = from_behind(filtered, "seg", 1)
    with jax.named_scope("base_to_points"):
        base_points = to_points(own_base, parts)
    with jax.named_scope("shift_base"):
        base_points = from_behind(base_points, "seg", 1)
    with jax.named_scope("state_to_points"):
        points = to_points(filtered, parts)
    with jax.named_scope("radial"):
        points = jnp.einsum("qr,rtz->qtz", radial_step, points, precision=EXACT)
        points = points + STEP_SIZE * base_points * points
        points = jnp.einsum("qr,rtz->qtz", radial_step, points, precision=EXACT)
    with jax.named_scope("state_to_radii"):
        carried = to_radii(points, parts)

    with jax.named_scope("closing_tables"):
        closing = lax.axis_index("seg") == first_segment[0] % lax.axis_size("seg")
        places_t = jnp.arange(count_t, dtype=jnp.int32)
        places_z = jnp.arange(count_z, dtype=jnp.int32)
        index_t = jnp.where(closing, (az_shift[0] - places_t) % count_t, places_t)
        index_z = jnp.where(closing, (places_z + ax_shift[0]) % count_z, places_z)
        last_t = jnp.take(table_t, index_t, axis=0)
        last_z = jnp.take(table_z, index_z, axis=0).T
    with jax.named_scope("last_filter"):
        carried = apply_filter(carried, last_t, last_z)
    return (carried - state)[None]


def solution(mesh):
    in_specs = (P("seg", "space", None, None), P("seg", "space", None, None), P(), P(), P(), P())
    out_specs = P("seg", "space", None, None)
    return jax.shard_map(shards, mesh=mesh, in_specs=in_specs, out_specs=out_specs, check_vma=False)
```

```python
import math

import jax
import jax.numpy as jnp
import ml_dtypes
import numpy as np
from jax import lax
from jax.experimental import pallas as pl
from jax.experimental.pallas import tpu as pltpu
from jax.sharding import PartitionSpec as P

STEP_SIZE = 0.25
VISCOUS_RATE = 1.5e-05
STAGGER = 0
TILE = 8


def filter_table(size):
    rows = np.arange(size)
    wave = np.where(rows == 0, 0, np.where(rows == 1, size // 2, rows // 2))
    angle = (wave[:, None] * rows[None, :] % size) * (2.0 * math.pi / size)
    sine = (rows % 2 == 1) & (rows >= 3)
    scale = np.where(rows < 2, math.sqrt(1.0 / size), math.sqrt(2.0 / size))
    table = scale[:, None] * np.where(sine[:, None], np.sin(angle), np.cos(angle))
    decay = np.exp(-VISCOUS_RATE * wave.astype(np.float64) ** 2)
    return (table.T @ (decay[:, None] * table)).astype(np.float32)


def split_constant(table):
    high = table.astype(ml_dtypes.bfloat16)
    return high, (table - high.astype(np.float32)).astype(ml_dtypes.bfloat16)


def split_array(array):
    high = lax.reduce_precision(array, 8, 7)
    return high.astype(jnp.bfloat16), (array - high).astype(jnp.bfloat16)


def split(value):
    high = value.astype(jnp.bfloat16)
    return high, (value - high.astype(jnp.float32)).astype(jnp.bfloat16)


def product(left, right):
    (left_high, left_low), (right_high, right_low) = left, right

    def dot(a, b):
        return jnp.dot(a, b, preferred_element_type=jnp.float32)

    return dot(left_high, right_high) + (dot(left_high, right_low) + dot(left_low, right_high))


def from_behind(block, axis, distance):
    devices = range(lax.axis_size(axis))
    route = [((i - distance) % len(devices), i) for i in devices]
    return lax.ppermute(block, axis, route)


def pack_pair(out_ref, first, second):
    parts = out_ref.shape[0]
    whole = parts * TILE
    count_z = first.shape[1]
    out_ref[:, 0:8, :] = first[:whole].reshape(parts, TILE, count_z)
    out_ref[:, 8:16, :] = second[:whole].reshape(parts, TILE, count_z)
    first = first[whole:].reshape(parts // 2, TILE, count_z)
    second = second[whole:].reshape(parts // 2, TILE, count_z)
    lower = lax.broadcasted_iota(jnp.int32, first.shape, 1) < TILE // 2
    even = jnp.where(lower, first, pltpu.roll(second, TILE // 2, 1))
    odd = jnp.where(lower, pltpu.roll(first, TILE // 2, 1), second)
    for k in range(parts // 2):
        out_ref[2 * k, 16:24, :] = even[k]
        out_ref[2 * k + 1, 16:24, :] = odd[k]


def unpack_pair(ref):
    parts, _, count_z = ref.shape
    whole = parts * TILE
    first = ref[:, 0:8, :].reshape(whole, count_z)
    second = ref[:, 8:16, :].reshape(whole, count_z)
    even = jnp.stack([ref[2 * k, 16:24, :] for k in range(parts // 2)])
    odd = jnp.stack([ref[2 * k + 1, 16:24, :] for k in range(parts // 2)])
    lower = lax.broadcasted_iota(jnp.int32, even.shape, 1) < TILE // 2
    first_rest = jnp.where(lower, even, pltpu.roll(odd, TILE // 2, 1)).reshape(whole // 2, count_z)
    second_rest = jnp.where(lower, pltpu.roll(even, TILE // 2, 1), odd).reshape(whole // 2, count_z)
    return jnp.concatenate([first, first_rest], 0), jnp.concatenate([second, second_rest], 0)


def filter_pair(first, second, table_t, table_z):
    count_z = first.shape[1]
    first = product(split(first), table_z)
    second = product(split(second), table_z)
    both = product(table_t, split(jnp.concatenate([first, second], 1)))
    return both[:, :count_z], both[:, count_z:]


def first_body(late_ref, field_ref, base_ref, th_ref, tl_ref, zh_ref, zl_ref, state_ref, base_out_ref):
    pack_pair(base_out_ref, base_ref[0], base_ref[1])
    forced = [field_ref[k] + STEP_SIZE * base_ref[k] * field_ref[k] for k in range(2)]
    table_t = (th_ref[...], tl_ref[...])
    table_z = (zh_ref[...], zl_ref[...])
    pack_pair(state_ref, *filter_pair(*forced, table_t, table_z))

    @pl.when(pl.program_id(0) == pl.num_programs(0) - 1)
    def _():
        pl.delay(late_ref[0])


def first_stage(field, base, table_t, table_z, parts, late):
    radii, count_t, count_z = field.shape
    plane = pl.BlockSpec((2, count_t, count_z), lambda p: (p, 0, 0))
    packed = pl.BlockSpec((parts, 24, count_z), lambda p: (0, p, 0))
    whole_t = pl.BlockSpec((count_t, count_t), lambda p: (0, 0))
    whole_z = pl.BlockSpec((count_z, count_z), lambda p: (0, 0))
    shape = jax.ShapeDtypeStruct((parts, 12 * radii, count_z), jnp.float32)
    return pl.pallas_call(
        first_body,
        out_shape=(shape, shape),
        grid=(radii // 2,),
        in_specs=[pl.BlockSpec(memory_space=pltpu.SMEM), plane, plane, whole_t, whole_t, whole_z, whole_z],
        out_specs=(packed, packed),
        name="first_stage",
    )(late, field, base, *table_t, *table_z)


def row_of(pair, half, point):
    return 24 * pair + (TILE * half + point if point < TILE else 2 * TILE + 4 * half + point - TILE)


def load_points(ref, point, parts):
    stride = ref.shape[0] // parts
    rows = [ref[pl.ds(row_of(p, e, point), parts, stride), :] for p in range(3) for e in range(2)]
    return jnp.concatenate(rows, 0)


def coefficient_body(base_ref, out_ref):
    parts = out_ref.shape[1] // 6
    for point in range(out_ref.shape[0]):
        out_ref[point] = 1.0 + STEP_SIZE * load_points(base_ref, point, parts)


def coefficient_stage(base, parts):
    rows, count_z = base.shape
    vmem = pl.BlockSpec(memory_space=pltpu.VMEM)
    return pl.pallas_call(
        coefficient_body,
        out_shape=jax.ShapeDtypeStruct((12, rows // 12, count_z), jnp.float32),
        in_specs=[vmem],
        out_specs=vmem,
        name="coefficient_stage",
    )(base)


def radial_body(state_ref, scale_ref, high_ref, low_ref, out_ref):
    parts = scale_ref.shape[1] // 6
    count_z = scale_ref.shape[2]
    stride = out_ref.shape[0] // parts
    mix = (high_ref[...], low_ref[...])
    for point in range(0, scale_ref.shape[0], 2):
        state = jnp.concatenate([load_points(state_ref, point + k, parts) for k in range(2)], 1)
        scale = jnp.concatenate([scale_ref[point + k] for k in range(2)], 1)
        state = product(mix, split(state)) * scale
        state = product(mix, split(state))
        for k in range(2):
            for p in range(3):
                for e in range(2):
                    radius = (2 * p + e) * parts
                    out_ref[pl.ds(row_of(p, e, point + k), parts, stride), :] = state[
                        radius : radius + parts, k * count_z : (k + 1) * count_z
                    ]


def radial_stage(state, scale, mix):
    vmem = pl.BlockSpec(memory_space=pltpu.VMEM)
    return pl.pallas_call(
        radial_body,
        out_shape=jax.ShapeDtypeStruct(state.shape, jnp.float32),
        in_specs=[vmem] * 4,
        out_specs=vmem,
        name="radial_stage",
    )(state, scale, *mix)


def last_body(state_ref, field_ref, th_ref, tl_ref, zh_ref, zl_ref, out_ref):
    table_t = (th_ref[...], tl_ref[...])
    table_z = (zh_ref[...], zl_ref[...])
    first, second = filter_pair(*unpack_pair(state_ref), table_t, table_z)
    out_ref[0] = first - field_ref[0]
    out_ref[1] = second - field_ref[1]


def last_stage(state, field, table_t, table_z, parts):
    radii, count_t, count_z = field.shape
    plane = pl.BlockSpec((2, count_t, count_z), lambda p: (p, 0, 0))
    packed = pl.BlockSpec((parts, 24, count_z), lambda p: (0, p, 0))
    whole_t = pl.BlockSpec((count_t, count_t), lambda p: (0, 0))
    whole_z = pl.BlockSpec((count_z, count_z), lambda p: (0, 0))
    return pl.pallas_call(
        last_body,
        out_shape=jax.ShapeDtypeStruct(field.shape, jnp.float32),
        grid=(radii // 2,),
        in_specs=[packed, plane, whole_t, whole_t, whole_z, whole_z],
        out_specs=plane,
        name="last_stage",
    )(state, field, *table_t, *table_z)


def swap(packed):
    return lax.all_to_all(packed, "space", 0, 0, tiled=True)


def shards(field, base, radial_step, az_shift, ax_shift, first_segment):
    state = field[0]
    count_t, count_z = state.shape[1:]
    parts = lax.axis_size("space")
    segment = lax.axis_index("seg")
    table_t = filter_table(count_t)
    table_z = filter_table(count_z)

    late = (STAGGER * (segment % 2)).astype(jnp.int32)[None]
    with jax.named_scope("first_filter"):
        filtered, base_packed = first_stage(
            state, base[0], split_constant(table_t), split_constant(table_z), parts, late
        )
    with jax.named_scope("shift_state"):
        filtered = from_behind(filtered, "seg", 1)
    with jax.named_scope("base_to_points"):
        base_points = swap(base_packed)
    with jax.named_scope("shift_base"):
        scale = coefficient_stage(base_points.reshape(-1, count_z), parts)
        scale = from_behind(scale, "seg", 1)
    with jax.named_scope("state_to_points"):
        points = swap(filtered)
    with jax.named_scope("radial"):
        mix = radial_step.reshape(parts, 6, parts, 6).transpose(1, 0, 3, 2).reshape(radial_step.shape)
        points = radial_stage(points.reshape(-1, count_z), scale, split_array(mix))
    with jax.named_scope("state_to_radii"):
        carried = swap(points.reshape(parts, -1, count_z))

    with jax.named_scope("closing_tables"):
        closing = segment == first_segment[0] % lax.axis_size("seg")
        places_t = jnp.arange(count_t, dtype=jnp.int32)
        places_z = jnp.arange(count_z, dtype=jnp.int32)
        index_t = jnp.where(closing, (az_shift[0] - places_t) % count_t, places_t)
        index_z = jnp.where(closing, (places_z + ax_shift[0]) % count_z, places_z)
        last_t = split_array(jnp.take(jnp.asarray(table_t), index_t, axis=0))
        last_z = split_array(jnp.take(jnp.asarray(table_z), index_z, axis=0).T)
    with jax.named_scope("last_filter"):
        return last_stage(carried, state, last_t, last_z, parts)[None]


def solution(mesh):
    in_specs = (P("seg", "space", None, None), P("seg", "space", None, None), P(), P(), P(), P())
    out_specs = P("seg", "space", None, None)
    return jax.shard_map(shards, mesh=mesh, in_specs=in_specs, out_specs=out_specs, check_vma=False)
```

```python
import math

import jax
import jax.numpy as jnp
import ml_dtypes
import numpy as np
from jax import lax
from jax.experimental import pallas as pl
from jax.experimental.pallas import tpu as pltpu
from jax.sharding import PartitionSpec as P

STEP_SIZE = 0.25
VISCOUS_RATE = 1.5e-05
STAGGER = 16000
TILE = 8


def filter_table(size):
    rows = np.arange(size)
    wave = np.where(rows == 0, 0, np.where(rows == 1, size // 2, rows // 2))
    angle = (wave[:, None] * rows[None, :] % size) * (2.0 * math.pi / size)
    sine = (rows % 2 == 1) & (rows >= 3)
    scale = np.where(rows < 2, math.sqrt(1.0 / size), math.sqrt(2.0 / size))
    table = scale[:, None] * np.where(sine[:, None], np.sin(angle), np.cos(angle))
    decay = np.exp(-VISCOUS_RATE * wave.astype(np.float64) ** 2)
    return (table.T @ (decay[:, None] * table)).astype(np.float32)


def split_constant(table):
    high = table.astype(ml_dtypes.bfloat16)
    return high, (table - high.astype(np.float32)).astype(ml_dtypes.bfloat16)


def split_array(array):
    high = lax.reduce_precision(array, 8, 7)
    return high.astype(jnp.bfloat16), (array - high).astype(jnp.bfloat16)


def split(value):
    high = value.astype(jnp.bfloat16)
    return high, (value - high.astype(jnp.float32)).astype(jnp.bfloat16)


def product(left, right):
    (left_high, left_low), (right_high, right_low) = left, right

    def dot(a, b):
        return jnp.dot(a, b, preferred_element_type=jnp.float32)

    return dot(left_high, right_high) + (dot(left_high, right_low) + dot(left_low, right_high))


def from_behind(block, axis, distance):
    devices = range(lax.axis_size(axis))
    route = [((i - distance) % len(devices), i) for i in devices]
    return lax.ppermute(block, axis, route)


def pack_pair(out_ref, first, second):
    parts = out_ref.shape[0]
    whole = parts * TILE
    count_z = first.shape[1]
    out_ref[:, 0:8, :] = first[:whole].reshape(parts, TILE, count_z)
    out_ref[:, 8:16, :] = second[:whole].reshape(parts, TILE, count_z)
    first = first[whole:].reshape(parts // 2, TILE, count_z)
    second = second[whole:].reshape(parts // 2, TILE, count_z)
    lower = lax.broadcasted_iota(jnp.int32, first.shape, 1) < TILE // 2
    even = jnp.where(lower, first, pltpu.roll(second, TILE // 2, 1))
    odd = jnp.where(lower, pltpu.roll(first, TILE // 2, 1), second)
    for k in range(parts // 2):
        out_ref[2 * k, 16:24, :] = even[k]
        out_ref[2 * k + 1, 16:24, :] = odd[k]


def unpack_pair(ref):
    parts, _, count_z = ref.shape
    whole = parts * TILE
    first = ref[:, 0:8, :].reshape(whole, count_z)
    second = ref[:, 8:16, :].reshape(whole, count_z)
    even = jnp.stack([ref[2 * k, 16:24, :] for k in range(parts // 2)])
    odd = jnp.stack([ref[2 * k + 1, 16:24, :] for k in range(parts // 2)])
    lower = lax.broadcasted_iota(jnp.int32, even.shape, 1) < TILE // 2
    first_rest = jnp.where(lower, even, pltpu.roll(odd, TILE // 2, 1)).reshape(whole // 2, count_z)
    second_rest = jnp.where(lower, pltpu.roll(even, TILE // 2, 1), odd).reshape(whole // 2, count_z)
    return jnp.concatenate([first, first_rest], 0), jnp.concatenate([second, second_rest], 0)


def filter_pair(first, second, table_t, table_z):
    count_z = first.shape[1]
    first = product(split(first), table_z)
    second = product(split(second), table_z)
    both = product(table_t, split(jnp.concatenate([first, second], 1)))
    return both[:, :count_z], both[:, count_z:]


def first_body(late_ref, field_ref, base_ref, th_ref, tl_ref, zh_ref, zl_ref, state_ref, base_out_ref):
    pack_pair(base_out_ref, base_ref[0], base_ref[1])
    forced = [field_ref[k] + STEP_SIZE * base_ref[k] * field_ref[k] for k in range(2)]
    table_t = (th_ref[...], tl_ref[...])
    table_z = (zh_ref[...], zl_ref[...])
    pack_pair(state_ref, *filter_pair(*forced, table_t, table_z))

    @pl.when(pl.program_id(0) == pl.num_programs(0) - 1)
    def _():
        pl.delay(late_ref[0])


def first_stage(field, base, table_t, table_z, parts, late):
    radii, count_t, count_z = field.shape
    plane = pl.BlockSpec((2, count_t, count_z), lambda p: (p, 0, 0))
    packed = pl.BlockSpec((parts, 24, count_z), lambda p: (0, p, 0))
    whole_t = pl.BlockSpec((count_t, count_t), lambda p: (0, 0))
    whole_z = pl.BlockSpec((count_z, count_z), lambda p: (0, 0))
    shape = jax.ShapeDtypeStruct((parts, 12 * radii, count_z), jnp.float32)
    return pl.pallas_call(
        first_body,
        out_shape=(shape, shape),
        grid=(radii // 2,),
        in_specs=[pl.BlockSpec(memory_space=pltpu.SMEM), plane, plane, whole_t, whole_t, whole_z, whole_z],
        out_specs=(packed, packed),
        name="first_stage",
    )(late, field, base, *table_t, *table_z)


def row_of(pair, half, point):
    return 24 * pair + (TILE * half + point if point < TILE else 2 * TILE + 4 * half + point - TILE)


def load_points(ref, point, parts):
    stride = ref.shape[0] // parts
    rows = [ref[pl.ds(row_of(p, e, point), parts, stride), :] for p in range(3) for e in range(2)]
    return jnp.concatenate(rows, 0)


def coefficient_body(base_ref, out_ref):
    parts = out_ref.shape[1] // 6
    for point in range(out_ref.shape[0]):
        out_ref[point] = 1.0 + STEP_SIZE * load_points(base_ref, point, parts)


def coefficient_stage(base, parts):
    rows, count_z = base.shape
    vmem = pl.BlockSpec(memory_space=pltpu.VMEM)
    return pl.pallas_call(
        coefficient_body,
        out_shape=jax.ShapeDtypeStruct((12, rows // 12, count_z), jnp.float32),
        in_specs=[vmem],
        out_specs=vmem,
        name="coefficient_stage",
    )(base)


def radial_body(state_ref, scale_ref, high_ref, low_ref, out_ref):
    parts = scale_ref.shape[1] // 6
    count_z = scale_ref.shape[2]
    stride = out_ref.shape[0] // parts
    mix = (high_ref[...], low_ref[...])
    for point in range(0, scale_ref.shape[0], 2):
        state = jnp.concatenate([load_points(state_ref, point + k, parts) for k in range(2)], 1)
        scale = jnp.concatenate([scale_ref[point + k] for k in range(2)], 1)
        state = product(mix, split(state)) * scale
        state = product(mix, split(state))
        for k in range(2):
            for p in range(3):
                for e in range(2):
                    radius = (2 * p + e) * parts
                    out_ref[pl.ds(row_of(p, e, point + k), parts, stride), :] = state[
                        radius : radius + parts, k * count_z : (k + 1) * count_z
                    ]


def radial_stage(state, scale, mix):
    vmem = pl.BlockSpec(memory_space=pltpu.VMEM)
    return pl.pallas_call(
        radial_body,
        out_shape=jax.ShapeDtypeStruct(state.shape, jnp.float32),
        in_specs=[vmem] * 4,
        out_specs=vmem,
        name="radial_stage",
    )(state, scale, *mix)


def last_body(state_ref, field_ref, th_ref, tl_ref, zh_ref, zl_ref, out_ref):
    table_t = (th_ref[...], tl_ref[...])
    table_z = (zh_ref[...], zl_ref[...])
    first, second = filter_pair(*unpack_pair(state_ref), table_t, table_z)
    out_ref[0] = first - field_ref[0]
    out_ref[1] = second - field_ref[1]


def last_stage(state, field, table_t, table_z, parts):
    radii, count_t, count_z = field.shape
    plane = pl.BlockSpec((2, count_t, count_z), lambda p: (p, 0, 0))
    packed = pl.BlockSpec((parts, 24, count_z), lambda p: (0, p, 0))
    whole_t = pl.BlockSpec((count_t, count_t), lambda p: (0, 0))
    whole_z = pl.BlockSpec((count_z, count_z), lambda p: (0, 0))
    return pl.pallas_call(
        last_body,
        out_shape=jax.ShapeDtypeStruct(field.shape, jnp.float32),
        grid=(radii // 2,),
        in_specs=[packed, plane, whole_t, whole_t, whole_z, whole_z],
        out_specs=plane,
        name="last_stage",
    )(state, field, *table_t, *table_z)


def swap(packed):
    return lax.all_to_all(packed, "space", 0, 0, tiled=True)


def shards(field, base, radial_step, az_shift, ax_shift, first_segment):
    state = field[0]
    count_t, count_z = state.shape[1:]
    parts = lax.axis_size("space")
    segment = lax.axis_index("seg")
    table_t = filter_table(count_t)
    table_z = filter_table(count_z)

    late = (STAGGER * (segment % 2)).astype(jnp.int32)[None]
    with jax.named_scope("first_filter"):
        filtered, base_packed = first_stage(
            state, base[0], split_constant(table_t), split_constant(table_z), parts, late
        )
    with jax.named_scope("shift_state"):
        filtered = from_behind(filtered, "seg", 1)
    with jax.named_scope("base_to_points"):
        base_points = swap(base_packed)
    with jax.named_scope("shift_base"):
        scale = coefficient_stage(base_points.reshape(-1, count_z), parts)
        scale = from_behind(scale, "seg", 1)
    with jax.named_scope("state_to_points"):
        points = swap(filtered)
    with jax.named_scope("radial"):
        mix = radial_step.reshape(parts, 6, parts, 6).transpose(1, 0, 3, 2).reshape(radial_step.shape)
        points = radial_stage(points.reshape(-1, count_z), scale, split_array(mix))
    with jax.named_scope("state_to_radii"):
        carried = swap(points.reshape(parts, -1, count_z))

    with jax.named_scope("closing_tables"):
        closing = segment == first_segment[0] % lax.axis_size("seg")
        places_t = jnp.arange(count_t, dtype=jnp.int32)
        places_z = jnp.arange(count_z, dtype=jnp.int32)
        index_t = jnp.where(closing, (az_shift[0] - places_t) % count_t, places_t)
        index_z = jnp.where(closing, (places_z + ax_shift[0]) % count_z, places_z)
        last_t = split_array(jnp.take(jnp.asarray(table_t), index_t, axis=0))
        last_z = split_array(jnp.take(jnp.asarray(table_z), index_z, axis=0).T)
    with jax.named_scope("last_filter"):
        return last_stage(carried, state, last_t, last_z, parts)[None]


def solution(mesh):
    in_specs = (P("seg", "space", None, None), P("seg", "space", None, None), P(), P(), P(), P())
    out_specs = P("seg", "space", None, None)
    return jax.shard_map(shards, mesh=mesh, in_specs=in_specs, out_specs=out_specs, check_vma=False)
```

```python
import math

import jax
import jax.numpy as jnp
import ml_dtypes
import numpy as np
from jax import lax
from jax.experimental import pallas as pl
from jax.experimental.pallas import tpu as pltpu
from jax.sharding import PartitionSpec as P

STEP_SIZE = 0.25
VISCOUS_RATE = 1.5e-05
STAGGER = 20000
TILE = 8


def filter_table(size):
    rows = np.arange(size)
    wave = np.where(rows == 0, 0, np.where(rows == 1, size // 2, rows // 2))
    angle = (wave[:, None] * rows[None, :] % size) * (2.0 * math.pi / size)
    sine = (rows % 2 == 1) & (rows >= 3)
    scale = np.where(rows < 2, math.sqrt(1.0 / size), math.sqrt(2.0 / size))
    table = scale[:, None] * np.where(sine[:, None], np.sin(angle), np.cos(angle))
    decay = np.exp(-VISCOUS_RATE * wave.astype(np.float64) ** 2)
    return (table.T @ (decay[:, None] * table)).astype(np.float32)


def split_constant(table):
    high = table.astype(ml_dtypes.bfloat16)
    return high, (table - high.astype(np.float32)).astype(ml_dtypes.bfloat16)


def split_array(array):
    high = lax.reduce_precision(array, 8, 7)
    return high.astype(jnp.bfloat16), (array - high).astype(jnp.bfloat16)


def split(value):
    high = value.astype(jnp.bfloat16)
    return high, (value - high.astype(jnp.float32)).astype(jnp.bfloat16)


def product(left, right):
    (left_high, left_low), (right_high, right_low) = left, right

    def dot(a, b):
        return jnp.dot(a, b, preferred_element_type=jnp.float32)

    return dot(left_high, right_high) + (dot(left_high, right_low) + dot(left_low, right_high))


def from_behind(block, axis, distance):
    devices = range(lax.axis_size(axis))
    route = [((i - distance) % len(devices), i) for i in devices]
    return lax.ppermute(block, axis, route)


def pack_pair(out_ref, first, second):
    parts = out_ref.shape[0]
    whole = parts * TILE
    count_z = first.shape[1]
    out_ref[:, 0:8, :] = first[:whole].reshape(parts, TILE, count_z)
    out_ref[:, 8:16, :] = second[:whole].reshape(parts, TILE, count_z)
    first = first[whole:].reshape(parts // 2, TILE, count_z)
    second = second[whole:].reshape(parts // 2, TILE, count_z)
    lower = lax.broadcasted_iota(jnp.int32, first.shape, 1) < TILE // 2
    even = jnp.where(lower, first, pltpu.roll(second, TILE // 2, 1))
    odd = jnp.where(lower, pltpu.roll(first, TILE // 2, 1), second)
    for k in range(parts // 2):
        out_ref[2 * k, 16:24, :] = even[k]
        out_ref[2 * k + 1, 16:24, :] = odd[k]


def unpack_pair(ref):
    parts, _, count_z = ref.shape
    whole = parts * TILE
    first = ref[:, 0:8, :].reshape(whole, count_z)
    second = ref[:, 8:16, :].reshape(whole, count_z)
    even = jnp.stack([ref[2 * k, 16:24, :] for k in range(parts // 2)])
    odd = jnp.stack([ref[2 * k + 1, 16:24, :] for k in range(parts // 2)])
    lower = lax.broadcasted_iota(jnp.int32, even.shape, 1) < TILE // 2
    first_rest = jnp.where(lower, even, pltpu.roll(odd, TILE // 2, 1)).reshape(whole // 2, count_z)
    second_rest = jnp.where(lower, pltpu.roll(even, TILE // 2, 1), odd).reshape(whole // 2, count_z)
    return jnp.concatenate([first, first_rest], 0), jnp.concatenate([second, second_rest], 0)


def filter_pair(first, second, table_t, table_z):
    count_z = first.shape[1]
    both = product(split(jnp.concatenate([first, second], 1)), table_z)
    both = product(table_t, split(both))
    return both[:, :count_z], both[:, count_z:]


def first_body(field_ref, base_ref, th_ref, tl_ref, zh_ref, zl_ref, state_ref, base_out_ref):
    pack_pair(base_out_ref, base_ref[0], base_ref[1])
    forced = [field_ref[k] + STEP_SIZE * base_ref[k] * field_ref[k] for k in range(2)]
    table_t = (th_ref[...], tl_ref[...])
    table_z = (zh_ref[...], zl_ref[...])
    pack_pair(state_ref, *filter_pair(*forced, table_t, table_z))


def first_stage(field, base, table_t, table_z, parts):
    radii, count_t, count_z = field.shape
    plane = pl.BlockSpec((2, count_t, count_z), lambda p: (p, 0, 0))
    packed = pl.BlockSpec((parts, 24, count_z), lambda p: (0, p, 0))
    whole_t = pl.BlockSpec((count_t, count_t), lambda p: (0, 0))
    whole_z = pl.BlockSpec((2 * count_z, 2 * count_z), lambda p: (0, 0))
    shape = jax.ShapeDtypeStruct((parts, 12 * radii, count_z), jnp.float32)
    return pl.pallas_call(
        first_body,
        out_shape=(shape, shape),
        grid=(radii // 2,),
        in_specs=[plane, plane, whole_t, whole_t, whole_z, whole_z],
        out_specs=(packed, packed),
        name="first_stage",
    )(field, base, *table_t, *table_z)


def hold_body(late_ref, block_ref, out_ref):
    pl.delay(late_ref[0])


def hold(block, late, weight):
    whole = pl.BlockSpec(memory_space=pl.ANY)
    return pl.pallas_call(
        hold_body,
        out_shape=jax.ShapeDtypeStruct(block.shape, block.dtype),
        in_specs=[pl.BlockSpec(memory_space=pltpu.SMEM), whole],
        out_specs=whole,
        input_output_aliases={1: 0},
        cost_estimate=pl.CostEstimate(flops=weight * 1000, transcendentals=0, bytes_accessed=0),
        name="hold",
    )(late, block)


def row_of(pair, half, point):
    return 24 * pair + (TILE * half + point if point < TILE else 2 * TILE + 4 * half + point - TILE)


def load_points(ref, point, parts):
    stride = ref.shape[0] // parts
    rows = [ref[pl.ds(row_of(p, e, point), parts, stride), :] for p in range(3) for e in range(2)]
    return jnp.concatenate(rows, 0)


def coefficient_body(base_ref, out_ref):
    parts = out_ref.shape[1] // 6
    for point in range(out_ref.shape[0]):
        out_ref[point] = 1.0 + STEP_SIZE * load_points(base_ref, point, parts)


def coefficient_stage(base, parts):
    rows, count_z = base.shape
    vmem = pl.BlockSpec(memory_space=pltpu.VMEM)
    return pl.pallas_call(
        coefficient_body,
        out_shape=jax.ShapeDtypeStruct((12, rows // 12, count_z), jnp.float32),
        in_specs=[vmem],
        out_specs=vmem,
        name="coefficient_stage",
    )(base)


def radial_body(state_ref, scale_ref, high_ref, low_ref, out_ref):
    parts = scale_ref.shape[1] // 6
    count_z = scale_ref.shape[2]
    stride = out_ref.shape[0] // parts
    mix = (high_ref[...], low_ref[...])
    for point in range(0, scale_ref.shape[0], 2):
        state = jnp.concatenate([load_points(state_ref, point + k, parts) for k in range(2)], 1)
        scale = jnp.concatenate([scale_ref[point + k] for k in range(2)], 1)
        state = product(mix, split(state)) * scale
        state = product(mix, split(state))
        for k in range(2):
            for p in range(3):
                for e in range(2):
                    radius = (2 * p + e) * parts
                    out_ref[pl.ds(row_of(p, e, point + k), parts, stride), :] = state[
                        radius : radius + parts, k * count_z : (k + 1) * count_z
                    ]


def radial_stage(state, scale, mix):
    vmem = pl.BlockSpec(memory_space=pltpu.VMEM)
    return pl.pallas_call(
        radial_body,
        out_shape=jax.ShapeDtypeStruct(state.shape, jnp.float32),
        in_specs=[vmem] * 4,
        out_specs=vmem,
        name="radial_stage",
    )(*in_vmem(state, scale, *mix))


def last_body(state_ref, field_ref, th_ref, tl_ref, zh_ref, zl_ref, out_ref, start, buffer, start_sems, sems):
    table_t = (th_ref[...], tl_ref[...])
    table_z = (zh_ref[...], zl_ref[...])
    pairs = start.shape[0] // 2
    rows = 12 * start.shape[0]
    state_ref = state_ref.reshape(state_ref.shape[0] // rows, rows, state_ref.shape[1])
    loads, copies = [], []
    for pair in range(pairs):
        planes = pl.ds(2 * pair, 2)
        loads.append(pltpu.make_async_copy(field_ref.at[planes], start.at[planes], start_sems.at[pair]))
        loads[-1].start()
    for pair in range(pairs):
        planes = pl.ds(2 * pair, 2)
        first, second = filter_pair(*unpack_pair(state_ref.at[:, pl.ds(24 * pair, 24), :]), table_t, table_z)
        loads[pair].wait()
        buffer[2 * pair] = first - start[2 * pair]
        buffer[2 * pair + 1] = second - start[2 * pair + 1]
        copies.append(pltpu.make_async_copy(buffer.at[planes], out_ref.at[planes], sems.at[pair]))
        copies[-1].start()
    for copy in copies:
        copy.wait()


def in_vmem(*arrays):
    return [pltpu.with_memory_space_constraint(array, pltpu.VMEM) for array in arrays]


def last_stage(state, field, table_t, table_z):
    vmem = pl.BlockSpec(memory_space=pltpu.VMEM)
    whole = pl.BlockSpec(memory_space=pl.ANY)
    (state,) = in_vmem(state)
    return pl.pallas_call(
        last_body,
        out_shape=jax.ShapeDtypeStruct(field.shape, jnp.float32),
        in_specs=[vmem, whole, vmem, vmem, vmem, vmem],
        out_specs=whole,
        scratch_shapes=[
            pltpu.VMEM(field.shape, jnp.float32),
            pltpu.VMEM(field.shape, jnp.float32),
            pltpu.SemaphoreType.DMA((field.shape[0] // 2,)),
            pltpu.SemaphoreType.DMA((field.shape[0] // 2,)),
        ],
        name="last_stage",
    )(state, field, *in_vmem(*table_t, *table_z))


def swap(packed):
    return lax.all_to_all(packed, "space", 0, 0, tiled=True)


def shards(field, base, radial_step, az_shift, ax_shift, first_segment):
    state = field[0]
    count_t, count_z = state.shape[1:]
    parts = lax.axis_size("space")
    segment = lax.axis_index("seg")
    table_t = filter_table(count_t)
    table_z = filter_table(count_z)

    late = (STAGGER * ((segment + 1) // 2 % 2)).astype(jnp.int32)[None]
    with jax.named_scope("first_filter"):
        pair_z = np.kron(np.eye(2, dtype=np.float32), table_z)
        filtered, base_packed = first_stage(
            state, base[0], split_constant(table_t), split_constant(pair_z), parts
        )
    with jax.named_scope("shift_state"):
        filtered = from_behind(filtered, "seg", 1)
        filtered = hold(filtered, jnp.zeros_like(late), 1 << 30)
    with jax.named_scope("base_to_points"):
        base_points = swap(hold(base_packed, late, 0))
    with jax.named_scope("shift_base"):
        scale = coefficient_stage(base_points.reshape(-1, count_z), parts)
        scale = from_behind(scale, "seg", 1)
    with jax.named_scope("state_to_points"):
        points = swap(filtered)
    with jax.named_scope("radial"):
        mix = radial_step.reshape(parts, 6, parts, 6).transpose(1, 0, 3, 2).reshape(radial_step.shape)
        points = radial_stage(points.reshape(-1, count_z), scale, split_array(mix))
    with jax.named_scope("state_to_radii"):
        carried = swap(points.reshape(parts, -1, count_z))

    with jax.named_scope("closing_tables"):
        closing = segment == first_segment[0] % lax.axis_size("seg")
        places_t = jnp.arange(count_t, dtype=jnp.int32)
        places_z = jnp.arange(count_z, dtype=jnp.int32)
        index_t = jnp.where(closing, (az_shift[0] - places_t) % count_t, places_t)
        index_z = jnp.where(closing, (places_z + ax_shift[0]) % count_z, places_z)
        last_t = split_array(jnp.take(jnp.asarray(table_t), index_t, axis=0))
        last_z = jnp.take(jnp.asarray(table_z), index_z, axis=0).T
        last_z = split_array(jnp.kron(jnp.eye(2, dtype=jnp.float32), last_z))
    with jax.named_scope("last_filter"):
        return last_stage(carried.reshape(-1, count_z), state, last_t, last_z)[None]


def solution(mesh):
    in_specs = (P("seg", "space", None, None), P("seg", "space", None, None), P(), P(), P(), P())
    out_specs = P("seg", "space", None, None)
    return jax.shard_map(shards, mesh=mesh, in_specs=in_specs, out_specs=out_specs, check_vma=False)
```

```python
import math

import jax
import jax.numpy as jnp
import ml_dtypes
import numpy as np
from jax import lax
from jax.experimental import pallas as pl
from jax.experimental.pallas import tpu as pltpu
from jax.sharding import PartitionSpec as P

STEP_SIZE = 0.25
VISCOUS_RATE = 1.5e-05
STAGGER = 22000
TILE = 8


def filter_table(size):
    rows = np.arange(size)
    wave = np.where(rows == 0, 0, np.where(rows == 1, size // 2, rows // 2))
    angle = (wave[:, None] * rows[None, :] % size) * (2.0 * math.pi / size)
    sine = (rows % 2 == 1) & (rows >= 3)
    scale = np.where(rows < 2, math.sqrt(1.0 / size), math.sqrt(2.0 / size))
    table = scale[:, None] * np.where(sine[:, None], np.sin(angle), np.cos(angle))
    decay = np.exp(-VISCOUS_RATE * wave.astype(np.float64) ** 2)
    return table.T @ (decay[:, None] * table)


def halves(table):
    half = table.shape[0] // 2
    return np.concatenate([table[:, :half] + table[:, half:], table[:, :half] - table[:, half:]], 0) / 2


def split_constant(table):
    table = table.astype(np.float32)
    high = table.astype(ml_dtypes.bfloat16)
    return high, (table - high.astype(np.float32)).astype(ml_dtypes.bfloat16)


def split_array(array):
    high = lax.reduce_precision(array, 8, 7)
    return high.astype(jnp.bfloat16), (array - high).astype(jnp.bfloat16)


def split(value):
    high = value.astype(jnp.bfloat16)
    return high, (value - high.astype(jnp.float32)).astype(jnp.bfloat16)


def product(left, right):
    (left_high, left_low), (right_high, right_low) = left, right

    def dot(a, b):
        return jnp.dot(a, b, preferred_element_type=jnp.float32)

    return dot(left_high, right_high) + (dot(left_high, right_low) + dot(left_low, right_high))


def from_behind(block, axis, distance):
    devices = range(lax.axis_size(axis))
    route = [((i - distance) % len(devices), i) for i in devices]
    return lax.ppermute(block, axis, route)


def pack_pair(out_ref, first, second):
    parts = out_ref.shape[0]
    whole = parts * TILE
    count_z = first.shape[1]
    out_ref[:, 0:8, :] = first[:whole].reshape(parts, TILE, count_z)
    out_ref[:, 8:16, :] = second[:whole].reshape(parts, TILE, count_z)
    first = first[whole:].reshape(parts // 2, TILE, count_z)
    second = second[whole:].reshape(parts // 2, TILE, count_z)
    lower = lax.broadcasted_iota(jnp.int32, first.shape, 1) < TILE // 2
    even = jnp.where(lower, first, pltpu.roll(second, TILE // 2, 1))
    odd = jnp.where(lower, pltpu.roll(first, TILE // 2, 1), second)
    for k in range(parts // 2):
        out_ref[2 * k, 16:24, :] = even[k]
        out_ref[2 * k + 1, 16:24, :] = odd[k]


def unpack_pair(ref):
    parts, _, count_z = ref.shape
    whole = parts * TILE
    first = ref[:, 0:8, :].reshape(whole, count_z)
    second = ref[:, 8:16, :].reshape(whole, count_z)
    even = jnp.stack([ref[2 * k, 16:24, :] for k in range(parts // 2)])
    odd = jnp.stack([ref[2 * k + 1, 16:24, :] for k in range(parts // 2)])
    lower = lax.broadcasted_iota(jnp.int32, even.shape, 1) < TILE // 2
    first_rest = jnp.where(lower, even, pltpu.roll(odd, TILE // 2, 1)).reshape(whole // 2, count_z)
    second_rest = jnp.where(lower, pltpu.roll(even, TILE // 2, 1), odd).reshape(whole // 2, count_z)
    return jnp.concatenate([first, first_rest], 0), jnp.concatenate([second, second_rest], 0)


def filter_pair(first, second, table_t, table_z):
    count_z = first.shape[1]
    half = first.shape[0] // 2
    both = product(split(jnp.concatenate([first, second], 1)), table_z)
    even = product([table[:half] for table in table_t], split(both[:half] + both[half:]))
    odd = product([table[half:] for table in table_t], split(both[:half] - both[half:]))
    both = jnp.concatenate([even + odd, even - odd], 0)
    return both[:, :count_z], both[:, count_z:]


def first_body(field_ref, base_ref, th_ref, tl_ref, zh_ref, zl_ref, state_ref, base_out_ref):
    pack_pair(base_out_ref, base_ref[0], base_ref[1])
    forced = [field_ref[k] + STEP_SIZE * base_ref[k] * field_ref[k] for k in range(2)]
    table_t = (th_ref[...], tl_ref[...])
    table_z = (zh_ref[...], zl_ref[...])
    pack_pair(state_ref, *filter_pair(*forced, table_t, table_z))


def first_stage(field, base, table_t, table_z, parts):
    radii, count_t, count_z = field.shape
    plane = pl.BlockSpec((2, count_t, count_z), lambda p: (p, 0, 0))
    packed = pl.BlockSpec((parts, 24, count_z), lambda p: (0, p, 0))
    whole_t = pl.BlockSpec((count_t, count_t // 2), lambda p: (0, 0))
    whole_z = pl.BlockSpec((2 * count_z, 2 * count_z), lambda p: (0, 0))
    shape = jax.ShapeDtypeStruct((parts, 12 * radii, count_z), jnp.float32)
    return pl.pallas_call(
        first_body,
        out_shape=(shape, shape),
        grid=(radii // 2,),
        in_specs=[plane, plane, whole_t, whole_t, whole_z, whole_z],
        out_specs=(packed, packed),
        name="first_stage",
    )(field, base, *table_t, *table_z)


def hold_body(late_ref, block_ref, out_ref):
    pl.delay(late_ref[0])


def hold(block, late, weight):
    whole = pl.BlockSpec(memory_space=pl.ANY)
    return pl.pallas_call(
        hold_body,
        out_shape=jax.ShapeDtypeStruct(block.shape, block.dtype),
        in_specs=[pl.BlockSpec(memory_space=pltpu.SMEM), whole],
        out_specs=whole,
        input_output_aliases={1: 0},
        cost_estimate=pl.CostEstimate(flops=weight * 1000, transcendentals=0, bytes_accessed=0),
        name="hold",
    )(late, block)


def row_of(pair, half, point):
    return 24 * pair + (TILE * half + point if point < TILE else 2 * TILE + 4 * half + point - TILE)


def load_points(ref, point, parts):
    stride = ref.shape[0] // parts
    rows = [ref[pl.ds(row_of(p, e, point), parts, stride), :] for p in range(3) for e in range(2)]
    return jnp.concatenate(rows, 0)


def coefficient_body(base_ref, out_ref):
    parts = out_ref.shape[1] // 6
    for point in range(out_ref.shape[0]):
        out_ref[point] = 1.0 + STEP_SIZE * load_points(base_ref, point, parts)


def coefficient_stage(base, parts):
    rows, count_z = base.shape
    vmem = pl.BlockSpec(memory_space=pltpu.VMEM)
    return pl.pallas_call(
        coefficient_body,
        out_shape=jax.ShapeDtypeStruct((12, rows // 12, count_z), jnp.float32),
        in_specs=[vmem],
        out_specs=vmem,
        name="coefficient_stage",
    )(base)


def mix_body(mix_ref, order_ref, high_ref, low_ref):
    order = order_ref[...]
    for part, out_ref in zip(split(mix_ref[...]), (high_ref, low_ref)):
        part = lax.dot_general(order, part, (((1,), (0,)), ((), ())), preferred_element_type=jnp.float32)
        part = part.astype(jnp.bfloat16)
        part = lax.dot_general(part, order, (((1,), (1,)), ((), ())), preferred_element_type=jnp.float32)
        out_ref[...] = part.astype(jnp.bfloat16)


def mix_stage(mix, parts):
    size = mix.shape[0]
    order = np.eye(size)[np.arange(size).reshape(parts, -1).T.reshape(-1)].astype(ml_dtypes.bfloat16)
    vmem = pl.BlockSpec(memory_space=pltpu.VMEM)
    shape = pltpu.VMEM(mix.shape, jnp.bfloat16)
    return pl.pallas_call(
        mix_body,
        out_shape=(shape, shape),
        in_specs=[vmem] * 2,
        out_specs=(vmem, vmem),
        name="mix_stage",
    )(mix, order)


def radial_body(state_ref, scale_ref, high_ref, low_ref, out_ref):
    parts = scale_ref.shape[1] // 6
    count_z = scale_ref.shape[2]
    stride = out_ref.shape[0] // parts
    mix = (high_ref[...], low_ref[...])
    for point in range(0, scale_ref.shape[0], 2):
        state = jnp.concatenate([load_points(state_ref, point + k, parts) for k in range(2)], 1)
        scale = jnp.concatenate([scale_ref[point + k] for k in range(2)], 1)
        state = product(mix, split(state)) * scale
        state = product(mix, split(state))
        for k in range(2):
            for p in range(3):
                for e in range(2):
                    radius = (2 * p + e) * parts
                    out_ref[pl.ds(row_of(p, e, point + k), parts, stride), :] = state[
                        radius : radius + parts, k * count_z : (k + 1) * count_z
                    ]


def radial_stage(state, scale, mix):
    vmem = pl.BlockSpec(memory_space=pltpu.VMEM)
    return pl.pallas_call(
        radial_body,
        out_shape=jax.ShapeDtypeStruct(state.shape, jnp.float32),
        in_specs=[vmem] * 4,
        out_specs=vmem,
        name="radial_stage",
    )(*in_vmem(state, scale, *mix))


def last_body(state_ref, field_ref, th_ref, tl_ref, zh_ref, zl_ref, out_ref, start, buffer, start_sems, sems):
    table_t = (th_ref[...], tl_ref[...])
    table_z = (zh_ref[...], zl_ref[...])
    pairs = start.shape[0] // 2
    rows = 12 * start.shape[0]
    state_ref = state_ref.reshape(state_ref.shape[0] // rows, rows, state_ref.shape[1])
    loads, copies = [], []
    for pair in range(pairs):
        planes = pl.ds(2 * pair, 2)
        loads.append(pltpu.make_async_copy(field_ref.at[planes], start.at[planes], start_sems.at[pair]))
        loads[-1].start()
    for pair in range(pairs):
        planes = pl.ds(2 * pair, 2)
        first, second = filter_pair(*unpack_pair(state_ref.at[:, pl.ds(24 * pair, 24), :]), table_t, table_z)
        loads[pair].wait()
        buffer[2 * pair] = first - start[2 * pair]
        buffer[2 * pair + 1] = second - start[2 * pair + 1]
        copies.append(pltpu.make_async_copy(buffer.at[planes], out_ref.at[planes], sems.at[pair]))
        copies[-1].start()
    for copy in copies:
        copy.wait()


def in_vmem(*arrays):
    return [pltpu.with_memory_space_constraint(array, pltpu.VMEM) for array in arrays]


def last_stage(state, field, table_t, table_z):
    vmem = pl.BlockSpec(memory_space=pltpu.VMEM)
    whole = pl.BlockSpec(memory_space=pl.ANY)
    (state,) = in_vmem(state)
    return pl.pallas_call(
        last_body,
        out_shape=jax.ShapeDtypeStruct(field.shape, jnp.float32),
        in_specs=[vmem, whole, vmem, vmem, vmem, vmem],
        out_specs=whole,
        scratch_shapes=[
            pltpu.VMEM(field.shape, jnp.float32),
            pltpu.VMEM(field.shape, jnp.float32),
            pltpu.SemaphoreType.DMA((field.shape[0] // 2,)),
            pltpu.SemaphoreType.DMA((field.shape[0] // 2,)),
        ],
        name="last_stage",
    )(state, field, *in_vmem(*table_t, *table_z))


def swap(packed):
    return lax.all_to_all(packed, "space", 0, 0, tiled=True)


def shards(field, base, radial_step, az_shift, ax_shift, first_segment):
    state = field[0]
    count_t, count_z = state.shape[1:]
    parts = lax.axis_size("space")
    segment = lax.axis_index("seg")
    table_t = filter_table(count_t)
    table_z = filter_table(count_z)

    late = (STAGGER * ((segment + 1) // 2 % 2)).astype(jnp.int32)[None]
    with jax.named_scope("first_filter"):
        pair_z = np.kron(np.eye(2), table_z)
        rows = np.arange(count_t // 2)
        half_t = split_constant(halves(table_t)[np.concatenate([rows, count_t + rows])])
        filtered, base_packed = first_stage(
            state, base[0], half_t, split_constant(pair_z), parts
        )
    with jax.named_scope("shift_state"):
        filtered = from_behind(filtered, "seg", 1)
        filtered = hold(filtered, jnp.zeros_like(late), 1 << 30)
    with jax.named_scope("base_to_points"):
        base_points = swap(hold(base_packed, late, 0))
    with jax.named_scope("shift_base"):
        scale = coefficient_stage(base_points.reshape(-1, count_z), parts)
        scale = from_behind(scale, "seg", 1)
    with jax.named_scope("state_to_points"):
        points = swap(filtered)
    with jax.named_scope("radial"):
        points = radial_stage(points.reshape(-1, count_z), scale, mix_stage(radial_step, parts))
    with jax.named_scope("state_to_radii"):
        carried = swap(points.reshape(parts, -1, count_z))

    with jax.named_scope("closing_tables"):
        closing = segment == first_segment[0] % lax.axis_size("seg")
        places_t = jnp.arange(count_t, dtype=jnp.int32)
        places_z = jnp.arange(count_z, dtype=jnp.int32)
        places_t = places_t[: count_t // 2]
        index_t = jnp.where(closing, (az_shift[0] - places_t) % count_t, places_t)
        index_t = jnp.concatenate([index_t, count_t + index_t])
        index_z = jnp.where(closing, (places_z + ax_shift[0]) % count_z, places_z)
        last_t = split_array(jnp.take(jnp.asarray(halves(table_t).astype(np.float32)), index_t, axis=0))
        last_z = jnp.take(jnp.asarray(table_z.astype(np.float32)), index_z, axis=0).T
        last_z = split_array(jnp.kron(jnp.eye(2, dtype=jnp.float32), last_z))
    with jax.named_scope("last_filter"):
        return last_stage(carried.reshape(-1, count_z), state, last_t, last_z)[None]


def solution(mesh):
    in_specs = (P("seg", "space", None, None), P("seg", "space", None, None), P(), P(), P(), P())
    out_specs = P("seg", "space", None, None)
    return jax.shard_map(shards, mesh=mesh, in_specs=in_specs, out_specs=out_specs, check_vma=False)
```

```python
import math

import jax
import jax.numpy as jnp
import ml_dtypes
import numpy as np
from jax import lax
from jax.experimental import pallas as pl
from jax.experimental.pallas import tpu as pltpu
from jax.sharding import PartitionSpec as P

STEP_SIZE = 0.25
VISCOUS_RATE = 1.5e-05
STAGGER = 25000
TILE = 8


def filter_table(size):
    rows = np.arange(size)
    wave = np.where(rows == 0, 0, np.where(rows == 1, size // 2, rows // 2))
    angle = (wave[:, None] * rows[None, :] % size) * (2.0 * math.pi / size)
    sine = (rows % 2 == 1) & (rows >= 3)
    scale = np.where(rows < 2, math.sqrt(1.0 / size), math.sqrt(2.0 / size))
    table = scale[:, None] * np.where(sine[:, None], np.sin(angle), np.cos(angle))
    decay = np.exp(-VISCOUS_RATE * wave.astype(np.float64) ** 2)
    return table.T @ (decay[:, None] * table)


def halves(table):
    half = table.shape[0] // 2
    return np.concatenate([table[:, :half] + table[:, half:], table[:, :half] - table[:, half:]], 0) / 2


def split_constant(table):
    table = table.astype(np.float32)
    high = table.astype(ml_dtypes.bfloat16)
    return high, (table - high.astype(np.float32)).astype(ml_dtypes.bfloat16)


def split_array(array):
    high = lax.reduce_precision(array, 8, 7)
    return high.astype(jnp.bfloat16), (array - high).astype(jnp.bfloat16)


def split(value):
    high = value.astype(jnp.bfloat16)
    return high, (value - high.astype(jnp.float32)).astype(jnp.bfloat16)


def product(left, right):
    (left_high, left_low), (right_high, right_low) = left, right

    def dot(a, b):
        return jnp.dot(a, b, preferred_element_type=jnp.float32)

    return dot(left_high, right_high) + (dot(left_high, right_low) + dot(left_low, right_high))


def from_behind(block, axis, distance):
    devices = range(lax.axis_size(axis))
    route = [((i - distance) % len(devices), i) for i in devices]
    return lax.ppermute(block, axis, route)


def pack_pair(out_ref, first, second):
    parts = out_ref.shape[0]
    whole = parts * TILE
    count_z = first.shape[1]
    out_ref[:, 0:8, :] = first[:whole].reshape(parts, TILE, count_z)
    out_ref[:, 8:16, :] = second[:whole].reshape(parts, TILE, count_z)
    first = first[whole:].reshape(parts // 2, TILE, count_z)
    second = second[whole:].reshape(parts // 2, TILE, count_z)
    lower = lax.broadcasted_iota(jnp.int32, first.shape, 1) < TILE // 2
    even = jnp.where(lower, first, pltpu.roll(second, TILE // 2, 1))
    odd = jnp.where(lower, pltpu.roll(first, TILE // 2, 1), second)
    for k in range(parts // 2):
        out_ref[2 * k, 16:24, :] = even[k]
        out_ref[2 * k + 1, 16:24, :] = odd[k]


def unpack_pair(ref):
    parts, _, count_z = ref.shape
    whole = parts * TILE
    first = ref[:, 0:8, :].reshape(whole, count_z)
    second = ref[:, 8:16, :].reshape(whole, count_z)
    even = jnp.stack([ref[2 * k, 16:24, :] for k in range(parts // 2)])
    odd = jnp.stack([ref[2 * k + 1, 16:24, :] for k in range(parts // 2)])
    lower = lax.broadcasted_iota(jnp.int32, even.shape, 1) < TILE // 2
    first_rest = jnp.where(lower, even, pltpu.roll(odd, TILE // 2, 1)).reshape(whole // 2, count_z)
    second_rest = jnp.where(lower, pltpu.roll(even, TILE // 2, 1), odd).reshape(whole // 2, count_z)
    return jnp.concatenate([first, first_rest], 0), jnp.concatenate([second, second_rest], 0)


def filter_pair(first, second, table_t, table_z):
    count_z = first.shape[1]
    half = first.shape[0] // 2
    both = product(split(jnp.concatenate([first, second], 1)), table_z)
    even = product([table[:half] for table in table_t], split(both[:half] + both[half:]))
    odd = product([table[half:] for table in table_t], split(both[:half] - both[half:]))
    both = jnp.concatenate([even + odd, even - odd], 0)
    return both[:, :count_z], both[:, count_z:]


def pack_body(late_ref, base_ref, out_ref):
    pack_pair(out_ref, base_ref[0], base_ref[1])

    @pl.when(pl.program_id(0) == pl.num_programs(0) - 1)
    def _():
        pl.delay(late_ref[0])


def pack_stage(base, parts, late):
    radii, count_t, count_z = base.shape
    return pl.pallas_call(
        pack_body,
        out_shape=jax.ShapeDtypeStruct((parts, 12 * radii, count_z), jnp.float32),
        grid=(radii // 2,),
        in_specs=[
            pl.BlockSpec(memory_space=pltpu.SMEM),
            pl.BlockSpec((2, count_t, count_z), lambda p: (p, 0, 0)),
        ],
        out_specs=pl.BlockSpec((parts, 24, count_z), lambda p: (0, p, 0)),
        name="pack_stage",
    )(late, base)


def first_body(field_ref, base_ref, th_ref, tl_ref, zh_ref, zl_ref, state_ref):
    forced = [field_ref[k] + STEP_SIZE * base_ref[k] * field_ref[k] for k in range(2)]
    table_t = (th_ref[...], tl_ref[...])
    table_z = (zh_ref[...], zl_ref[...])
    pack_pair(state_ref, *filter_pair(*forced, table_t, table_z))


def first_stage(field, base, table_t, table_z, parts):
    radii, count_t, count_z = field.shape
    plane = pl.BlockSpec((2, count_t, count_z), lambda p: (p, 0, 0))
    whole_t = pl.BlockSpec((count_t, count_t // 2), lambda p: (0, 0))
    whole_z = pl.BlockSpec((2 * count_z, 2 * count_z), lambda p: (0, 0))
    return pl.pallas_call(
        first_body,
        out_shape=jax.ShapeDtypeStruct((parts, 12 * radii, count_z), jnp.float32),
        grid=(radii // 2,),
        in_specs=[plane, plane, whole_t, whole_t, whole_z, whole_z],
        out_specs=pl.BlockSpec((parts, 24, count_z), lambda p: (0, p, 0)),
        name="first_stage",
    )(field, base, *table_t, *table_z)


def row_of(pair, half, point):
    return 24 * pair + (TILE * half + point if point < TILE else 2 * TILE + 4 * half + point - TILE)


def load_points(ref, point, parts):
    stride = ref.shape[0] // parts
    rows = [ref[pl.ds(row_of(p, e, point), parts, stride), :] for p in range(3) for e in range(2)]
    return jnp.concatenate(rows, 0)


def coefficient_body(base_ref, out_ref):
    parts = out_ref.shape[1] // 6
    for point in range(out_ref.shape[0]):
        out_ref[point] = 1.0 + STEP_SIZE * load_points(base_ref, point, parts)


def coefficient_stage(base, parts):
    rows, count_z = base.shape
    vmem = pl.BlockSpec(memory_space=pltpu.VMEM)
    return pl.pallas_call(
        coefficient_body,
        out_shape=jax.ShapeDtypeStruct((12, rows // 12, count_z), jnp.float32),
        in_specs=[vmem],
        out_specs=vmem,
        name="coefficient_stage",
    )(base)


def mix_body(mix_ref, order_ref, high_ref, low_ref):
    order = order_ref[...]
    for part, out_ref in zip(split(mix_ref[...]), (high_ref, low_ref)):
        part = lax.dot_general(order, part, (((1,), (0,)), ((), ())), preferred_element_type=jnp.float32)
        part = part.astype(jnp.bfloat16)
        part = lax.dot_general(part, order, (((1,), (1,)), ((), ())), preferred_element_type=jnp.float32)
        out_ref[...] = part.astype(jnp.bfloat16)


def mix_stage(mix, parts):
    size = mix.shape[0]
    order = np.eye(size)[np.arange(size).reshape(parts, -1).T.reshape(-1)].astype(ml_dtypes.bfloat16)
    vmem = pl.BlockSpec(memory_space=pltpu.VMEM)
    shape = pltpu.VMEM(mix.shape, jnp.bfloat16)
    return pl.pallas_call(
        mix_body,
        out_shape=(shape, shape),
        in_specs=[vmem] * 2,
        out_specs=(vmem, vmem),
        name="mix_stage",
    )(mix, order)


def radial_body(state_ref, scale_ref, high_ref, low_ref, out_ref):
    parts = scale_ref.shape[1] // 6
    count_z = scale_ref.shape[2]
    stride = out_ref.shape[0] // parts
    mix = (high_ref[...], low_ref[...])
    for point in range(0, scale_ref.shape[0], 2):
        state = jnp.concatenate([load_points(state_ref, point + k, parts) for k in range(2)], 1)
        scale = jnp.concatenate([scale_ref[point + k] for k in range(2)], 1)
        state = product(mix, split(state)) * scale
        state = product(mix, split(state))
        for k in range(2):
            for p in range(3):
                for e in range(2):
                    radius = (2 * p + e) * parts
                    out_ref[pl.ds(row_of(p, e, point + k), parts, stride), :] = state[
                        radius : radius + parts, k * count_z : (k + 1) * count_z
                    ]


def radial_stage(state, scale, mix):
    vmem = pl.BlockSpec(memory_space=pltpu.VMEM)
    return pl.pallas_call(
        radial_body,
        out_shape=jax.ShapeDtypeStruct(state.shape, jnp.float32),
        in_specs=[vmem] * 4,
        out_specs=vmem,
        name="radial_stage",
    )(*in_vmem(state, scale, *mix))


def last_body(state_ref, field_ref, th_ref, tl_ref, zh_ref, zl_ref, out_ref, start, buffer, start_sems, sems):
    table_t = (th_ref[...], tl_ref[...])
    table_z = (zh_ref[...], zl_ref[...])
    pairs = start.shape[0] // 2
    rows = 12 * start.shape[0]
    state_ref = state_ref.reshape(state_ref.shape[0] // rows, rows, state_ref.shape[1])
    loads, copies = [], []
    for pair in range(pairs):
        planes = pl.ds(2 * pair, 2)
        loads.append(pltpu.make_async_copy(field_ref.at[planes], start.at[planes], start_sems.at[pair]))
        loads[-1].start()
    for pair in range(pairs):
        planes = pl.ds(2 * pair, 2)
        first, second = filter_pair(*unpack_pair(state_ref.at[:, pl.ds(24 * pair, 24), :]), table_t, table_z)
        loads[pair].wait()
        buffer[2 * pair] = first - start[2 * pair]
        buffer[2 * pair + 1] = second - start[2 * pair + 1]
        copies.append(pltpu.make_async_copy(buffer.at[planes], out_ref.at[planes], sems.at[pair]))
        copies[-1].start()
    for copy in copies:
        copy.wait()


def in_vmem(*arrays):
    return [pltpu.with_memory_space_constraint(array, pltpu.VMEM) for array in arrays]


def last_stage(state, field, table_t, table_z):
    vmem = pl.BlockSpec(memory_space=pltpu.VMEM)
    whole = pl.BlockSpec(memory_space=pl.ANY)
    (state,) = in_vmem(state)
    return pl.pallas_call(
        last_body,
        out_shape=jax.ShapeDtypeStruct(field.shape, jnp.float32),
        in_specs=[vmem, whole, vmem, vmem, vmem, vmem],
        out_specs=whole,
        scratch_shapes=[
            pltpu.VMEM(field.shape, jnp.float32),
            pltpu.VMEM(field.shape, jnp.float32),
            pltpu.SemaphoreType.DMA((field.shape[0] // 2,)),
            pltpu.SemaphoreType.DMA((field.shape[0] // 2,)),
        ],
        name="last_stage",
    )(state, field, *in_vmem(*table_t, *table_z))


def swap(packed):
    return lax.all_to_all(packed, "space", 0, 0, tiled=True)


def shards(field, base, radial_step, az_shift, ax_shift, first_segment):
    state = field[0]
    count_t, count_z = state.shape[1:]
    parts = lax.axis_size("space")
    segment = lax.axis_index("seg")
    table_t = filter_table(count_t)
    table_z = filter_table(count_z)

    late = (STAGGER * ((segment + 1) // 2 % 2)).astype(jnp.int32)[None]
    with jax.named_scope("pack_base"):
        base_packed = pack_stage(base[0], parts, late)
    with jax.named_scope("base_to_points"):
        base_points = swap(base_packed)
    with jax.named_scope("first_filter"):
        pair_z = np.kron(np.eye(2), table_z)
        rows = np.arange(count_t // 2)
        half_t = split_constant(halves(table_t)[np.concatenate([rows, count_t + rows])])
        filtered = first_stage(state, base[0], half_t, split_constant(pair_z), parts)
    with jax.named_scope("shift_state"):
        filtered = from_behind(filtered, "seg", 1)
    with jax.named_scope("shift_base"):
        scale = coefficient_stage(base_points.reshape(-1, count_z), parts)
        scale = from_behind(scale, "seg", 1)
    with jax.named_scope("state_to_points"):
        points = swap(filtered)
    with jax.named_scope("radial"):
        points = radial_stage(points.reshape(-1, count_z), scale, mix_stage(radial_step, parts))
    with jax.named_scope("state_to_radii"):
        carried = swap(points.reshape(parts, -1, count_z))

    with jax.named_scope("closing_tables"):
        closing = segment == first_segment[0] % lax.axis_size("seg")
        places_t = jnp.arange(count_t, dtype=jnp.int32)
        places_z = jnp.arange(count_z, dtype=jnp.int32)
        places_t = places_t[: count_t // 2]
        index_t = jnp.where(closing, (az_shift[0] - places_t) % count_t, places_t)
        index_t = jnp.concatenate([index_t, count_t + index_t])
        index_z = jnp.where(closing, (places_z + ax_shift[0]) % count_z, places_z)
        last_t = split_array(jnp.take(jnp.asarray(halves(table_t).astype(np.float32)), index_t, axis=0))
        last_z = jnp.take(jnp.asarray(table_z.astype(np.float32)), index_z, axis=0).T
        last_z = split_array(jnp.kron(jnp.eye(2, dtype=jnp.float32), last_z))
    with jax.named_scope("last_filter"):
        return last_stage(carried.reshape(-1, count_z), state, last_t, last_z)[None]


def solution(mesh):
    in_specs = (P("seg", "space", None, None), P("seg", "space", None, None), P(), P(), P(), P())
    out_specs = P("seg", "space", None, None)
    return jax.shard_map(shards, mesh=mesh, in_specs=in_specs, out_specs=out_specs, check_vma=False)
```

```python
import math

import jax
import jax.numpy as jnp
import ml_dtypes
import numpy as np
from jax import lax
from jax.experimental import pallas as pl
from jax.experimental.pallas import tpu as pltpu
from jax.sharding import PartitionSpec as P

STEP_SIZE = 0.25
VISCOUS_RATE = 1.5e-05
STAGGER = 25000
TILE = 8


def filter_table(size):
    rows = np.arange(size)
    wave = np.where(rows == 0, 0, np.where(rows == 1, size // 2, rows // 2))
    angle = (wave[:, None] * rows[None, :] % size) * (2.0 * math.pi / size)
    sine = (rows % 2 == 1) & (rows >= 3)
    scale = np.where(rows < 2, math.sqrt(1.0 / size), math.sqrt(2.0 / size))
    table = scale[:, None] * np.where(sine[:, None], np.sin(angle), np.cos(angle))
    decay = np.exp(-VISCOUS_RATE * wave.astype(np.float64) ** 2)
    return table.T @ (decay[:, None] * table)


def halves(table):
    half = table.shape[0] // 2
    return np.concatenate([table[:, :half] + table[:, half:], table[:, :half] - table[:, half:]], 0) / 2


def split_constant(table):
    table = table.astype(np.float32)
    high = table.astype(ml_dtypes.bfloat16)
    return high, (table - high.astype(np.float32)).astype(ml_dtypes.bfloat16)


def split_array(array):
    high = lax.reduce_precision(array, 8, 7)
    return high.astype(jnp.bfloat16), (array - high).astype(jnp.bfloat16)


def split(value):
    high = value.astype(jnp.bfloat16)
    return high, (value - high.astype(jnp.float32)).astype(jnp.bfloat16)


def product(left, right):
    (left_high, left_low), (right_high, right_low) = left, right

    def dot(a, b):
        return jnp.dot(a, b, preferred_element_type=jnp.float32)

    return dot(left_high, right_high) + (dot(left_high, right_low) + dot(left_low, right_high))


def from_behind(block, axis, distance):
    devices = range(lax.axis_size(axis))
    route = [((i - distance) % len(devices), i) for i in devices]
    return lax.ppermute(block, axis, route)


def pack_pair(out_ref, first, second):
    parts = out_ref.shape[0]
    whole = parts * TILE
    count_z = first.shape[1]
    out_ref[:, 0:8, :] = first[:whole].reshape(parts, TILE, count_z)
    out_ref[:, 8:16, :] = second[:whole].reshape(parts, TILE, count_z)
    first = first[whole:].reshape(parts // 2, TILE, count_z)
    second = second[whole:].reshape(parts // 2, TILE, count_z)
    lower = lax.broadcasted_iota(jnp.int32, first.shape, 1) < TILE // 2
    even = jnp.where(lower, first, pltpu.roll(second, TILE // 2, 1))
    odd = jnp.where(lower, pltpu.roll(first, TILE // 2, 1), second)
    for k in range(parts // 2):
        out_ref[2 * k, 16:24, :] = even[k]
        out_ref[2 * k + 1, 16:24, :] = odd[k]


def unpack_pair(ref):
    parts, _, count_z = ref.shape
    whole = parts * TILE
    first = ref[:, 0:8, :].reshape(whole, count_z)
    second = ref[:, 8:16, :].reshape(whole, count_z)
    even = jnp.stack([ref[2 * k, 16:24, :] for k in range(parts // 2)])
    odd = jnp.stack([ref[2 * k + 1, 16:24, :] for k in range(parts // 2)])
    lower = lax.broadcasted_iota(jnp.int32, even.shape, 1) < TILE // 2
    first_rest = jnp.where(lower, even, pltpu.roll(odd, TILE // 2, 1)).reshape(whole // 2, count_z)
    second_rest = jnp.where(lower, pltpu.roll(even, TILE // 2, 1), odd).reshape(whole // 2, count_z)
    return jnp.concatenate([first, first_rest], 0), jnp.concatenate([second, second_rest], 0)


def filter_pair(first, second, table_t, table_z):
    count_z = first.shape[1]
    half = first.shape[0] // 2
    both = product(split(jnp.concatenate([first, second], 1)), table_z)
    even = product([table[:half] for table in table_t], split(both[:half] + both[half:]))
    odd = product([table[half:] for table in table_t], split(both[:half] - both[half:]))
    both = jnp.concatenate([even + odd, even - odd], 0)
    return both[:, :count_z], both[:, count_z:]


def pack_body(late_ref, base_ref, out_ref, start, packed, start_sems, sems):
    loads, copies = [], []
    for pair in range(start.shape[0] // 2):
        planes = pl.ds(2 * pair, 2)
        loads.append(pltpu.make_async_copy(base_ref.at[planes], start.at[planes], start_sems.at[pair]))
        loads[-1].start()
    for pair, load in enumerate(loads):
        rows = pl.ds(24 * pair, 24)
        load.wait()
        pack_pair(packed.at[:, rows, :], start[2 * pair], start[2 * pair + 1])
        copies.append(pltpu.make_async_copy(packed.at[:, rows, :], out_ref.at[:, rows, :], sems.at[pair]))
        copies[-1].start()
    pl.delay(late_ref[0])
    for copy in copies:
        copy.wait()


def pack_stage(base, parts, late):
    radii, count_t, count_z = base.shape
    shape = (parts, 12 * radii, count_z)
    hbm = pl.BlockSpec(memory_space=pltpu.HBM)
    return pl.pallas_call(
        pack_body,
        out_shape=jax.ShapeDtypeStruct(shape, jnp.float32),
        in_specs=[pl.BlockSpec(memory_space=pltpu.SMEM), hbm],
        out_specs=hbm,
        scratch_shapes=[
            pltpu.VMEM(base.shape, jnp.float32),
            pltpu.VMEM(shape, jnp.float32),
            pltpu.SemaphoreType.DMA((radii // 2,)),
            pltpu.SemaphoreType.DMA((radii // 2,)),
        ],
        name="pack_stage",
    )(late, base)


def first_body(field_ref, base_ref, th_ref, tl_ref, zh_ref, zl_ref, state_ref):
    forced = [field_ref[k] + STEP_SIZE * base_ref[k] * field_ref[k] for k in range(2)]
    table_t = (th_ref[...], tl_ref[...])
    table_z = (zh_ref[...], zl_ref[...])
    pack_pair(state_ref, *filter_pair(*forced, table_t, table_z))


def first_stage(field, base, table_t, table_z, parts):
    radii, count_t, count_z = field.shape
    plane = pl.BlockSpec((2, count_t, count_z), lambda p: (p, 0, 0))
    whole_t = pl.BlockSpec((count_t, count_t // 2), lambda p: (0, 0))
    whole_z = pl.BlockSpec((2 * count_z, 2 * count_z), lambda p: (0, 0))
    return pl.pallas_call(
        first_body,
        out_shape=jax.ShapeDtypeStruct((parts, 12 * radii, count_z), jnp.float32),
        grid=(radii // 2,),
        in_specs=[plane, plane, whole_t, whole_t, whole_z, whole_z],
        out_specs=pl.BlockSpec((parts, 24, count_z), lambda p: (0, p, 0)),
        name="first_stage",
    )(field, base, *table_t, *table_z)


def row_of(pair, half, point):
    return 24 * pair + (TILE * half + point if point < TILE else 2 * TILE + 4 * half + point - TILE)


def load_points(ref, point, parts):
    stride = ref.shape[0] // parts
    rows = [ref[pl.ds(row_of(p, e, point), parts, stride), :] for p in range(3) for e in range(2)]
    return jnp.concatenate(rows, 0)


def coefficient_body(base_ref, out_ref):
    parts = out_ref.shape[1] // 6
    for point in range(out_ref.shape[0]):
        out_ref[point] = 1.0 + STEP_SIZE * load_points(base_ref, point, parts)


def coefficient_stage(base, parts):
    rows, count_z = base.shape
    vmem = pl.BlockSpec(memory_space=pltpu.VMEM)
    return pl.pallas_call(
        coefficient_body,
        out_shape=jax.ShapeDtypeStruct((12, rows // 12, count_z), jnp.float32),
        in_specs=[vmem],
        out_specs=vmem,
        name="coefficient_stage",
    )(base)


def mix_body(mix_ref, order_ref, high_ref, low_ref):
    order = order_ref[...]
    for part, out_ref in zip(split(mix_ref[...]), (high_ref, low_ref)):
        part = lax.dot_general(order, part, (((1,), (0,)), ((), ())), preferred_element_type=jnp.float32)
        part = part.astype(jnp.bfloat16)
        part = lax.dot_general(part, order, (((1,), (1,)), ((), ())), preferred_element_type=jnp.float32)
        out_ref[...] = part.astype(jnp.bfloat16)


def mix_stage(mix, parts):
    size = mix.shape[0]
    order = np.eye(size)[np.arange(size).reshape(parts, -1).T.reshape(-1)].astype(ml_dtypes.bfloat16)
    vmem = pl.BlockSpec(memory_space=pltpu.VMEM)
    shape = pltpu.VMEM(mix.shape, jnp.bfloat16)
    return pl.pallas_call(
        mix_body,
        out_shape=(shape, shape),
        in_specs=[vmem] * 2,
        out_specs=(vmem, vmem),
        name="mix_stage",
    )(mix, order)


def radial_body(state_ref, scale_ref, high_ref, low_ref, out_ref):
    parts = scale_ref.shape[1] // 6
    count_z = scale_ref.shape[2]
    stride = out_ref.shape[0] // parts
    mix = (high_ref[...], low_ref[...])
    for point in range(0, scale_ref.shape[0], 2):
        state = jnp.concatenate([load_points(state_ref, point + k, parts) for k in range(2)], 1)
        scale = jnp.concatenate([scale_ref[point + k] for k in range(2)], 1)
        state = product(mix, split(state)) * scale
        state = product(mix, split(state))
        for k in range(2):
            for p in range(3):
                for e in range(2):
                    radius = (2 * p + e) * parts
                    out_ref[pl.ds(row_of(p, e, point + k), parts, stride), :] = state[
                        radius : radius + parts, k * count_z : (k + 1) * count_z
                    ]


def radial_stage(state, scale, mix):
    vmem = pl.BlockSpec(memory_space=pltpu.VMEM)
    return pl.pallas_call(
        radial_body,
        out_shape=jax.ShapeDtypeStruct(state.shape, jnp.float32),
        in_specs=[vmem] * 4,
        out_specs=vmem,
        name="radial_stage",
    )(*in_vmem(state, scale, *mix))


def last_body(state_ref, field_ref, th_ref, tl_ref, zh_ref, zl_ref, out_ref, start, buffer, start_sems, sems):
    table_t = (th_ref[...], tl_ref[...])
    table_z = (zh_ref[...], zl_ref[...])
    pairs = start.shape[0] // 2
    rows = 12 * start.shape[0]
    state_ref = state_ref.reshape(state_ref.shape[0] // rows, rows, state_ref.shape[1])
    loads, copies = [], []
    for pair in range(pairs):
        planes = pl.ds(2 * pair, 2)
        loads.append(pltpu.make_async_copy(field_ref.at[planes], start.at[planes], start_sems.at[pair]))
        loads[-1].start()
    for pair in range(pairs):
        planes = pl.ds(2 * pair, 2)
        first, second = filter_pair(*unpack_pair(state_ref.at[:, pl.ds(24 * pair, 24), :]), table_t, table_z)
        loads[pair].wait()
        buffer[2 * pair] = first - start[2 * pair]
        buffer[2 * pair + 1] = second - start[2 * pair + 1]
        copies.append(pltpu.make_async_copy(buffer.at[planes], out_ref.at[planes], sems.at[pair]))
        copies[-1].start()
    for copy in copies:
        copy.wait()


def in_vmem(*arrays):
    return [pltpu.with_memory_space_constraint(array, pltpu.VMEM) for array in arrays]


def last_stage(state, field, table_t, table_z):
    vmem = pl.BlockSpec(memory_space=pltpu.VMEM)
    whole = pl.BlockSpec(memory_space=pl.ANY)
    (state,) = in_vmem(state)
    return pl.pallas_call(
        last_body,
        out_shape=jax.ShapeDtypeStruct(field.shape, jnp.float32),
        in_specs=[vmem, whole, vmem, vmem, vmem, vmem],
        out_specs=whole,
        scratch_shapes=[
            pltpu.VMEM(field.shape, jnp.float32),
            pltpu.VMEM(field.shape, jnp.float32),
            pltpu.SemaphoreType.DMA((field.shape[0] // 2,)),
            pltpu.SemaphoreType.DMA((field.shape[0] // 2,)),
        ],
        name="last_stage",
    )(state, field, *in_vmem(*table_t, *table_z))


def swap(packed):
    return lax.all_to_all(packed, "space", 0, 0, tiled=True)


def shards(field, base, radial_step, az_shift, ax_shift, first_segment):
    state = field[0]
    count_t, count_z = state.shape[1:]
    parts = lax.axis_size("space")
    segment = lax.axis_index("seg")
    table_t = filter_table(count_t)
    table_z = filter_table(count_z)

    late = (STAGGER * ((segment + 1) // 2 % 2)).astype(jnp.int32)[None]
    with jax.named_scope("pack_base"):
        base_packed = pack_stage(base[0], parts, late)
    with jax.named_scope("base_to_points"):
        base_points = swap(base_packed)
    with jax.named_scope("first_filter"):
        pair_z = np.kron(np.eye(2), table_z)
        rows = np.arange(count_t // 2)
        half_t = split_constant(halves(table_t)[np.concatenate([rows, count_t + rows])])
        filtered = first_stage(state, base[0], half_t, split_constant(pair_z), parts)
    with jax.named_scope("shift_state"):
        filtered = from_behind(filtered, "seg", 1)
    with jax.named_scope("shift_base"):
        scale = coefficient_stage(base_points.reshape(-1, count_z), parts)
        scale = from_behind(scale, "seg", 1)
    with jax.named_scope("state_to_points"):
        points = swap(filtered)
    with jax.named_scope("radial"):
        points = radial_stage(points.reshape(-1, count_z), scale, mix_stage(radial_step, parts))
    with jax.named_scope("state_to_radii"):
        carried = swap(points.reshape(parts, -1, count_z))

    with jax.named_scope("closing_tables"):
        closing = segment == first_segment[0] % lax.axis_size("seg")
        places_t = jnp.arange(count_t, dtype=jnp.int32)
        places_z = jnp.arange(count_z, dtype=jnp.int32)
        places_t = places_t[: count_t // 2]
        index_t = jnp.where(closing, (az_shift[0] - places_t) % count_t, places_t)
        index_t = jnp.concatenate([index_t, count_t + index_t])
        index_z = jnp.where(closing, (places_z + ax_shift[0]) % count_z, places_z)
        last_t = split_array(jnp.take(jnp.asarray(halves(table_t).astype(np.float32)), index_t, axis=0))
        last_z = jnp.take(jnp.asarray(table_z.astype(np.float32)), index_z, axis=0).T
        last_z = split_array(jnp.kron(jnp.eye(2, dtype=jnp.float32), last_z))
    with jax.named_scope("last_filter"):
        return last_stage(carried.reshape(-1, count_z), state, last_t, last_z)[None]


def solution(mesh):
    in_specs = (P("seg", "space", None, None), P("seg", "space", None, None), P(), P(), P(), P())
    out_specs = P("seg", "space", None, None)
    return jax.shard_map(shards, mesh=mesh, in_specs=in_specs, out_specs=out_specs, check_vma=False)
```

```python
import math

import jax
import jax.numpy as jnp
import ml_dtypes
import numpy as np
from jax import lax
from jax.experimental import pallas as pl
from jax.experimental.pallas import tpu as pltpu
from jax.sharding import PartitionSpec as P

STEP_SIZE = 0.25
VISCOUS_RATE = 1.5e-05
STAGGER = 25000
TILE = 8


def filter_table(size):
    rows = np.arange(size)
    wave = np.where(rows == 0, 0, np.where(rows == 1, size // 2, rows // 2))
    angle = (wave[:, None] * rows[None, :] % size) * (2.0 * math.pi / size)
    sine = (rows % 2 == 1) & (rows >= 3)
    scale = np.where(rows < 2, math.sqrt(1.0 / size), math.sqrt(2.0 / size))
    table = scale[:, None] * np.where(sine[:, None], np.sin(angle), np.cos(angle))
    decay = np.exp(-VISCOUS_RATE * wave.astype(np.float64) ** 2)
    return table.T @ (decay[:, None] * table)


def halves(table):
    half = table.shape[0] // 2
    return np.concatenate([table[:, :half] + table[:, half:], table[:, :half] - table[:, half:]], 0) / 2


def split_constant(table):
    table = table.astype(np.float32)
    high = table.astype(ml_dtypes.bfloat16)
    return high, (table - high.astype(np.float32)).astype(ml_dtypes.bfloat16)


def split_array(array):
    high = lax.reduce_precision(array, 8, 7)
    return high.astype(jnp.bfloat16), (array - high).astype(jnp.bfloat16)


def split(value):
    high = value.astype(jnp.bfloat16)
    return high, (value - high.astype(jnp.float32)).astype(jnp.bfloat16)


def product(left, right):
    (left_high, left_low), (right_high, right_low) = left, right

    def dot(a, b):
        return jnp.dot(a, b, preferred_element_type=jnp.float32)

    return dot(left_high, right_high) + (dot(left_high, right_low) + dot(left_low, right_high))


def wide(high, low):
    return jnp.concatenate([jnp.concatenate([high, low], 1), jnp.concatenate([high, jnp.zeros_like(low)], 1)], 0)


def from_behind(block, axis, distance):
    devices = range(lax.axis_size(axis))
    route = [((i - distance) % len(devices), i) for i in devices]
    return lax.ppermute(block, axis, route)


def pack_pair(out_ref, first, second):
    parts = out_ref.shape[0]
    whole = parts * TILE
    count_z = first.shape[1]
    out_ref[:, 0:8, :] = first[:whole].reshape(parts, TILE, count_z)
    out_ref[:, 8:16, :] = second[:whole].reshape(parts, TILE, count_z)
    first = first[whole:].reshape(parts // 2, TILE, count_z)
    second = second[whole:].reshape(parts // 2, TILE, count_z)
    lower = lax.broadcasted_iota(jnp.int32, first.shape, 1) < TILE // 2
    even = jnp.where(lower, first, pltpu.roll(second, TILE // 2, 1))
    odd = jnp.where(lower, pltpu.roll(first, TILE // 2, 1), second)
    for k in range(parts // 2):
        out_ref[2 * k, 16:24, :] = even[k]
        out_ref[2 * k + 1, 16:24, :] = odd[k]


def unpack_pair(ref):
    parts, _, count_z = ref.shape
    whole = parts * TILE
    first = ref[:, 0:8, :].reshape(whole, count_z)
    second = ref[:, 8:16, :].reshape(whole, count_z)
    even = jnp.stack([ref[2 * k, 16:24, :] for k in range(parts // 2)])
    odd = jnp.stack([ref[2 * k + 1, 16:24, :] for k in range(parts // 2)])
    lower = lax.broadcasted_iota(jnp.int32, even.shape, 1) < TILE // 2
    first_rest = jnp.where(lower, even, pltpu.roll(odd, TILE // 2, 1)).reshape(whole // 2, count_z)
    second_rest = jnp.where(lower, pltpu.roll(even, TILE // 2, 1), odd).reshape(whole // 2, count_z)
    return jnp.concatenate([first, first_rest], 0), jnp.concatenate([second, second_rest], 0)


def filter_pair(first, second, table_t, table_z):
    count_z = first.shape[1]
    half = first.shape[0] // 2
    both = []
    for plane in (first, second):
        plane = jnp.dot(jnp.concatenate(split(plane), 1), table_z, preferred_element_type=jnp.float32)
        both.append(plane[:, :count_z] + plane[:, count_z:])
    both = jnp.concatenate(both, 1)
    even = product([table[:half] for table in table_t], split(both[:half] + both[half:]))
    odd = product([table[half:] for table in table_t], split(both[:half] - both[half:]))
    both = jnp.concatenate([even + odd, even - odd], 0)
    return both[:, :count_z], both[:, count_z:]


def pack_body(late_ref, base_ref, out_ref, start, packed, start_sems, sems):
    loads, copies = [], []
    for pair in range(start.shape[0] // 2):
        planes = pl.ds(2 * pair, 2)
        loads.append(pltpu.make_async_copy(base_ref.at[planes], start.at[planes], start_sems.at[pair]))
        loads[-1].start()
    for pair, load in enumerate(loads):
        rows = pl.ds(24 * pair, 24)
        load.wait()
        pack_pair(packed.at[:, rows, :], start[2 * pair], start[2 * pair + 1])
        copies.append(pltpu.make_async_copy(packed.at[:, rows, :], out_ref.at[:, rows, :], sems.at[pair]))
        copies[-1].start()
    pl.delay(late_ref[0])
    for copy in copies:
        copy.wait()


def pack_stage(base, parts, late):
    radii, count_t, count_z = base.shape
    shape = (parts, 12 * radii, count_z)
    hbm = pl.BlockSpec(memory_space=pltpu.HBM)
    return pl.pallas_call(
        pack_body,
        out_shape=jax.ShapeDtypeStruct(shape, jnp.float32),
        in_specs=[pl.BlockSpec(memory_space=pltpu.SMEM), hbm],
        out_specs=hbm,
        scratch_shapes=[
            pltpu.VMEM(base.shape, jnp.float32),
            pltpu.VMEM(shape, jnp.float32),
            pltpu.SemaphoreType.DMA((radii // 2,)),
            pltpu.SemaphoreType.DMA((radii // 2,)),
        ],
        name="pack_stage",
    )(late, base)


def first_body(field_ref, base_ref, th_ref, tl_ref, z_ref, state_ref):
    forced = [field_ref[k] + STEP_SIZE * base_ref[k] * field_ref[k] for k in range(2)]
    table_t = (th_ref[...], tl_ref[...])
    table_z = z_ref[...]
    pack_pair(state_ref, *filter_pair(*forced, table_t, table_z))


def first_stage(field, base, table_t, table_z, parts):
    radii, count_t, count_z = field.shape
    plane = pl.BlockSpec((2, count_t, count_z), lambda p: (p, 0, 0))
    whole_t = pl.BlockSpec((count_t, count_t // 2), lambda p: (0, 0))
    whole_z = pl.BlockSpec((2 * count_z, 2 * count_z), lambda p: (0, 0))
    return pl.pallas_call(
        first_body,
        out_shape=jax.ShapeDtypeStruct((parts, 12 * radii, count_z), jnp.float32),
        grid=(radii // 2,),
        in_specs=[plane, plane, whole_t, whole_t, whole_z],
        out_specs=pl.BlockSpec((parts, 24, count_z), lambda p: (0, p, 0)),
        name="first_stage",
    )(field, base, *table_t, table_z)


def row_of(pair, half, point):
    return 24 * pair + (TILE * half + point if point < TILE else 2 * TILE + 4 * half + point - TILE)


def load_points(ref, point, parts):
    stride = ref.shape[0] // parts
    rows = [ref[pl.ds(row_of(p, e, point), parts, stride), :] for p in range(3) for e in range(2)]
    return jnp.concatenate(rows, 0)


def coefficient_body(base_ref, out_ref):
    parts = out_ref.shape[1] // 6
    for point in range(out_ref.shape[0]):
        out_ref[point] = 1.0 + STEP_SIZE * load_points(base_ref, point, parts)


def coefficient_stage(base, parts):
    rows, count_z = base.shape
    vmem = pl.BlockSpec(memory_space=pltpu.VMEM)
    return pl.pallas_call(
        coefficient_body,
        out_shape=jax.ShapeDtypeStruct((12, rows // 12, count_z), jnp.float32),
        in_specs=[vmem],
        out_specs=vmem,
        name="coefficient_stage",
    )(base)


def mix_body(mix_ref, order_ref, high_ref, low_ref):
    order = order_ref[...]
    for part, out_ref in zip(split(mix_ref[...]), (high_ref, low_ref)):
        part = lax.dot_general(order, part, (((1,), (0,)), ((), ())), preferred_element_type=jnp.float32)
        part = part.astype(jnp.bfloat16)
        part = lax.dot_general(part, order, (((1,), (1,)), ((), ())), preferred_element_type=jnp.float32)
        out_ref[...] = part.astype(jnp.bfloat16)


def mix_stage(mix, parts):
    size = mix.shape[0]
    order = np.eye(size)[np.arange(size).reshape(parts, -1).T.reshape(-1)].astype(ml_dtypes.bfloat16)
    vmem = pl.BlockSpec(memory_space=pltpu.VMEM)
    shape = pltpu.VMEM(mix.shape, jnp.bfloat16)
    return pl.pallas_call(
        mix_body,
        out_shape=(shape, shape),
        in_specs=[vmem] * 2,
        out_specs=(vmem, vmem),
        name="mix_stage",
    )(mix, order)


def radial_body(state_ref, scale_ref, high_ref, low_ref, out_ref):
    parts = scale_ref.shape[1] // 6
    count_z = scale_ref.shape[2]
    stride = out_ref.shape[0] // parts
    mix = (high_ref[...], low_ref[...])
    for point in range(0, scale_ref.shape[0], 2):
        state = jnp.concatenate([load_points(state_ref, point + k, parts) for k in range(2)], 1)
        scale = jnp.concatenate([scale_ref[point + k] for k in range(2)], 1)
        state = product(mix, split(state)) * scale
        state = product(mix, split(state))
        for k in range(2):
            for p in range(3):
                for e in range(2):
                    radius = (2 * p + e) * parts
                    out_ref[pl.ds(row_of(p, e, point + k), parts, stride), :] = state[
                        radius : radius + parts, k * count_z : (k + 1) * count_z
                    ]


def radial_stage(state, scale, mix):
    vmem = pl.BlockSpec(memory_space=pltpu.VMEM)
    return pl.pallas_call(
        radial_body,
        out_shape=jax.ShapeDtypeStruct(state.shape, jnp.float32),
        in_specs=[vmem] * 4,
        out_specs=vmem,
        name="radial_stage",
    )(*in_vmem(state, scale, *mix))


def last_body(state_ref, field_ref, th_ref, tl_ref, z_ref, out_ref, start, buffer, start_sems, sems):
    table_t = (th_ref[...], tl_ref[...])
    table_z = z_ref[...]
    pairs = start.shape[0] // 2
    rows = 12 * start.shape[0]
    state_ref = state_ref.reshape(state_ref.shape[0] // rows, rows, state_ref.shape[1])
    loads, copies = [], []
    for pair in range(pairs):
        planes = pl.ds(2 * pair, 2)
        loads.append(pltpu.make_async_copy(field_ref.at[planes], start.at[planes], start_sems.at[pair]))
        loads[-1].start()
    for pair in range(pairs):
        planes = pl.ds(2 * pair, 2)
        first, second = filter_pair(*unpack_pair(state_ref.at[:, pl.ds(24 * pair, 24), :]), table_t, table_z)
        loads[pair].wait()
        buffer[2 * pair] = first - start[2 * pair]
        buffer[2 * pair + 1] = second - start[2 * pair + 1]
        copies.append(pltpu.make_async_copy(buffer.at[planes], out_ref.at[planes], sems.at[pair]))
        copies[-1].start()
    for copy in copies:
        copy.wait()


def in_vmem(*arrays):
    return [pltpu.with_memory_space_constraint(array, pltpu.VMEM) for array in arrays]


def last_stage(state, field, table_t, table_z):
    vmem = pl.BlockSpec(memory_space=pltpu.VMEM)
    whole = pl.BlockSpec(memory_space=pl.ANY)
    (state,) = in_vmem(state)
    return pl.pallas_call(
        last_body,
        out_shape=jax.ShapeDtypeStruct(field.shape, jnp.float32),
        in_specs=[vmem, whole, vmem, vmem, vmem],
        out_specs=whole,
        scratch_shapes=[
            pltpu.VMEM(field.shape, jnp.float32),
            pltpu.VMEM(field.shape, jnp.float32),
            pltpu.SemaphoreType.DMA((field.shape[0] // 2,)),
            pltpu.SemaphoreType.DMA((field.shape[0] // 2,)),
        ],
        name="last_stage",
    )(state, field, *in_vmem(*table_t, table_z))


def swap(packed):
    return lax.all_to_all(packed, "space", 0, 0, tiled=True)


def shards(field, base, radial_step, az_shift, ax_shift, first_segment):
    state = field[0]
    count_t, count_z = state.shape[1:]
    parts = lax.axis_size("space")
    segment = lax.axis_index("seg")
    table_t = filter_table(count_t)
    table_z = filter_table(count_z)

    late = (STAGGER * ((segment + 1) // 2 % 2)).astype(jnp.int32)[None]
    with jax.named_scope("pack_base"):
        base_packed = pack_stage(base[0], parts, late)
    with jax.named_scope("base_to_points"):
        base_points = swap(base_packed)
    with jax.named_scope("first_filter"):
        high, low = split_constant(table_z)
        wide_z = np.block([[high, low], [high, np.zeros_like(low)]])
        rows = np.arange(count_t // 2)
        half_t = split_constant(halves(table_t)[np.concatenate([rows, count_t + rows])])
        filtered = first_stage(state, base[0], half_t, wide_z, parts)
    with jax.named_scope("shift_state"):
        filtered = from_behind(filtered, "seg", 1)
    with jax.named_scope("shift_base"):
        scale = coefficient_stage(base_points.reshape(-1, count_z), parts)
        scale = from_behind(scale, "seg", 1)
    with jax.named_scope("state_to_points"):
        points = swap(filtered)
    with jax.named_scope("radial"):
        points = radial_stage(points.reshape(-1, count_z), scale, mix_stage(radial_step, parts))
    with jax.named_scope("state_to_radii"):
        carried = swap(points.reshape(parts, -1, count_z))

    with jax.named_scope("closing_tables"):
        closing = segment == first_segment[0] % lax.axis_size("seg")
        places_t = jnp.arange(count_t, dtype=jnp.int32)
        places_z = jnp.arange(count_z, dtype=jnp.int32)
        places_t = places_t[: count_t // 2]
        index_t = jnp.where(closing, (az_shift[0] - places_t) % count_t, places_t)
        index_t = jnp.concatenate([index_t, count_t + index_t])
        index_z = jnp.where(closing, (places_z + ax_shift[0]) % count_z, places_z)
        last_t = split_array(jnp.take(jnp.asarray(halves(table_t).astype(np.float32)), index_t, axis=0))
        last_z = jnp.take(jnp.asarray(table_z.astype(np.float32)), index_z, axis=0).T
        last_z = wide(*split_array(last_z))
    with jax.named_scope("last_filter"):
        return last_stage(carried.reshape(-1, count_z), state, last_t, last_z)[None]


def solution(mesh):
    in_specs = (P("seg", "space", None, None), P("seg", "space", None, None), P(), P(), P(), P())
    out_specs = P("seg", "space", None, None)
    return jax.shard_map(shards, mesh=mesh, in_specs=in_specs, out_specs=out_specs, check_vma=False)
```

```python
import math

import jax
import jax.numpy as jnp
import ml_dtypes
import numpy as np
from jax import lax
from jax.experimental import pallas as pl
from jax.experimental.pallas import tpu as pltpu
from jax.sharding import PartitionSpec as P

STEP_SIZE = 0.25
VISCOUS_RATE = 1.5e-05
STAGGER = 25000
TILE = 8


def filter_table(size):
    rows = np.arange(size)
    wave = np.where(rows == 0, 0, np.where(rows == 1, size // 2, rows // 2))
    angle = (wave[:, None] * rows[None, :] % size) * (2.0 * math.pi / size)
    sine = (rows % 2 == 1) & (rows >= 3)
    scale = np.where(rows < 2, math.sqrt(1.0 / size), math.sqrt(2.0 / size))
    table = scale[:, None] * np.where(sine[:, None], np.sin(angle), np.cos(angle))
    decay = np.exp(-VISCOUS_RATE * wave.astype(np.float64) ** 2)
    return table.T @ (decay[:, None] * table)


def halves(table):
    half = table.shape[0] // 2
    return np.concatenate([table[:, :half] + table[:, half:], table[:, :half] - table[:, half:]], 0) / 2


def split_constant(table):
    table = table.astype(np.float32)
    high = table.astype(ml_dtypes.bfloat16)
    return high, (table - high.astype(np.float32)).astype(ml_dtypes.bfloat16)


def split_array(array):
    high = lax.reduce_precision(array, 8, 7)
    return high.astype(jnp.bfloat16), (array - high).astype(jnp.bfloat16)


def split(value):
    high = value.astype(jnp.bfloat16)
    return high, (value - high.astype(jnp.float32)).astype(jnp.bfloat16)


def product(left, right):
    (left_high, left_low), (right_high, right_low) = left, right

    def dot(a, b):
        return jnp.dot(a, b, preferred_element_type=jnp.float32)

    return dot(left_high, right_high) + (dot(left_high, right_low) + dot(left_low, right_high))


def wide(high, low):
    return jnp.concatenate([jnp.concatenate([high, low], 1), jnp.concatenate([high, jnp.zeros_like(low)], 1)], 0)


def from_behind(block, axis, distance):
    devices = range(lax.axis_size(axis))
    route = [((i - distance) % len(devices), i) for i in devices]
    return lax.ppermute(block, axis, route)


def pack_pair(out_ref, first, second):
    parts = out_ref.shape[0]
    whole = parts * TILE
    count_z = first.shape[1]
    out_ref[:, 0:8, :] = first[:whole].reshape(parts, TILE, count_z)
    out_ref[:, 8:16, :] = second[:whole].reshape(parts, TILE, count_z)
    first = first[whole:].reshape(parts // 2, TILE, count_z)
    second = second[whole:].reshape(parts // 2, TILE, count_z)
    lower = lax.broadcasted_iota(jnp.int32, first.shape, 1) < TILE // 2
    even = jnp.where(lower, first, pltpu.roll(second, TILE // 2, 1))
    odd = jnp.where(lower, pltpu.roll(first, TILE // 2, 1), second)
    for k in range(parts // 2):
        out_ref[2 * k, 16:24, :] = even[k]
        out_ref[2 * k + 1, 16:24, :] = odd[k]


def unpack_pair(ref):
    parts, _, count_z = ref.shape
    whole = parts * TILE
    first = ref[:, 0:8, :].reshape(whole, count_z)
    second = ref[:, 8:16, :].reshape(whole, count_z)
    even = jnp.stack([ref[2 * k, 16:24, :] for k in range(parts // 2)])
    odd = jnp.stack([ref[2 * k + 1, 16:24, :] for k in range(parts // 2)])
    lower = lax.broadcasted_iota(jnp.int32, even.shape, 1) < TILE // 2
    first_rest = jnp.where(lower, even, pltpu.roll(odd, TILE // 2, 1)).reshape(whole // 2, count_z)
    second_rest = jnp.where(lower, pltpu.roll(even, TILE // 2, 1), odd).reshape(whole // 2, count_z)
    return jnp.concatenate([first, first_rest], 0), jnp.concatenate([second, second_rest], 0)


def filter_pair(first, second, table_t, table_z):
    count_z = first.shape[1]
    half = first.shape[0] // 2
    both = []
    for plane in (first, second):
        plane = jnp.dot(jnp.concatenate(split(plane), 1), table_z, preferred_element_type=jnp.float32)
        both.append(plane[:, :count_z] + plane[:, count_z:])
    both = jnp.concatenate(both, 1)
    even = product([table[:half] for table in table_t], split(both[:half] + both[half:]))
    odd = product([table[half:] for table in table_t], split(both[:half] - both[half:]))
    both = jnp.concatenate([even + odd, even - odd], 0)
    return both[:, :count_z], both[:, count_z:]


def pack_body(late_ref, base_ref, out_ref, start, packed, start_sems, sems):
    loads, copies = [], []
    for pair in range(start.shape[0] // 2):
        planes = pl.ds(2 * pair, 2)
        loads.append(pltpu.make_async_copy(base_ref.at[planes], start.at[planes], start_sems.at[pair]))
        loads[-1].start()
    for pair, load in enumerate(loads):
        rows = pl.ds(24 * pair, 24)
        load.wait()
        pack_pair(packed.at[:, rows, :], start[2 * pair], start[2 * pair + 1])
        copies.append(pltpu.make_async_copy(packed.at[:, rows, :], out_ref.at[:, rows, :], sems.at[pair]))
        copies[-1].start()
    pl.delay(late_ref[0])
    for copy in copies:
        copy.wait()


def pack_stage(base, parts, late):
    radii, count_t, count_z = base.shape
    shape = (parts, 12 * radii, count_z)
    hbm = pl.BlockSpec(memory_space=pltpu.HBM)
    return pl.pallas_call(
        pack_body,
        out_shape=jax.ShapeDtypeStruct(shape, jnp.float32),
        in_specs=[pl.BlockSpec(memory_space=pltpu.SMEM), hbm],
        out_specs=hbm,
        scratch_shapes=[
            pltpu.VMEM(base.shape, jnp.float32),
            pltpu.VMEM(shape, jnp.float32),
            pltpu.SemaphoreType.DMA((radii // 2,)),
            pltpu.SemaphoreType.DMA((radii // 2,)),
        ],
        name="pack_stage",
    )(late, base)


def first_body(field_ref, base_ref, th_ref, tl_ref, z_ref, state_ref):
    forced = [field_ref[k] + STEP_SIZE * base_ref[k] * field_ref[k] for k in range(2)]
    table_t = (th_ref[...], tl_ref[...])
    table_z = z_ref[...]
    pack_pair(state_ref, *filter_pair(*forced, table_t, table_z))


def first_stage(field, base, table_t, table_z, parts):
    radii, count_t, count_z = field.shape
    plane = pl.BlockSpec((2, count_t, count_z), lambda p: (p, 0, 0))
    whole_t = pl.BlockSpec((count_t, count_t // 2), lambda p: (0, 0))
    whole_z = pl.BlockSpec((2 * count_z, 2 * count_z), lambda p: (0, 0))
    return pl.pallas_call(
        first_body,
        out_shape=jax.ShapeDtypeStruct((parts, 12 * radii, count_z), jnp.float32),
        grid=(radii // 2,),
        in_specs=[plane, plane, whole_t, whole_t, whole_z],
        out_specs=pl.BlockSpec((parts, 24, count_z), lambda p: (0, p, 0)),
        name="first_stage",
    )(field, base, *table_t, table_z)


def row_of(pair, half, point):
    return 24 * pair + (TILE * half + point if point < TILE else 2 * TILE + 4 * half + point - TILE)


def load_points(ref, point, parts):
    stride = ref.shape[0] // parts
    rows = [ref[pl.ds(row_of(p, e, point), parts, stride), :] for p in range(3) for e in range(2)]
    return jnp.concatenate(rows, 0)


def coefficient_body(base_ref, out_ref):
    parts = out_ref.shape[1] // 6
    for point in range(out_ref.shape[0]):
        out_ref[point] = 1.0 + STEP_SIZE * load_points(base_ref, point, parts)


def coefficient_stage(base, parts):
    rows, count_z = base.shape
    vmem = pl.BlockSpec(memory_space=pltpu.VMEM)
    return pl.pallas_call(
        coefficient_body,
        out_shape=jax.ShapeDtypeStruct((12, rows // 12, count_z), jnp.float32),
        in_specs=[vmem],
        out_specs=vmem,
        name="coefficient_stage",
    )(base)


def mix_body(mix_ref, order_ref, high_ref, low_ref):
    order = order_ref[...]
    for part, out_ref in zip(split(mix_ref[...]), (high_ref, low_ref)):
        part = lax.dot_general(order, part, (((1,), (0,)), ((), ())), preferred_element_type=jnp.float32)
        part = part.astype(jnp.bfloat16)
        part = lax.dot_general(part, order, (((1,), (1,)), ((), ())), preferred_element_type=jnp.float32)
        out_ref[...] = part.astype(jnp.bfloat16)


def mix_stage(mix, parts):
    size = mix.shape[0]
    order = np.eye(size)[np.arange(size).reshape(parts, -1).T.reshape(-1)].astype(ml_dtypes.bfloat16)
    vmem = pl.BlockSpec(memory_space=pltpu.VMEM)
    shape = pltpu.VMEM(mix.shape, jnp.bfloat16)
    return pl.pallas_call(
        mix_body,
        out_shape=(shape, shape),
        in_specs=[vmem] * 2,
        out_specs=(vmem, vmem),
        name="mix_stage",
    )(mix, order)


def radial_body(state_ref, scale_ref, high_ref, low_ref, result_ref, out_ref, sems):
    parts = scale_ref.shape[1] // 6
    count_z = scale_ref.shape[2]
    stride = out_ref.shape[0] // parts
    mix = (high_ref[...], low_ref[...])
    blocks = out_ref.reshape(parts, stride, count_z)
    copies = []

    def send(first, rows):
        for p in range(3):
            window = pl.ds(24 * p + first, rows)
            copies.append(
                pltpu.make_async_copy(blocks.at[:, window, :], result_ref.at[:, window, :], sems.at[len(copies)])
            )
            copies[-1].start()

    for point in range(0, scale_ref.shape[0], 2):
        state = jnp.concatenate([load_points(state_ref, point + k, parts) for k in range(2)], 1)
        scale = jnp.concatenate([scale_ref[point + k] for k in range(2)], 1)
        state = product(mix, split(state)) * scale
        state = product(mix, split(state))
        for k in range(2):
            for p in range(3):
                for e in range(2):
                    radius = (2 * p + e) * parts
                    out_ref[pl.ds(row_of(p, e, point + k), parts, stride), :] = state[
                        radius : radius + parts, k * count_z : (k + 1) * count_z
                    ]
        if point + 2 == TILE:
            send(0, 2 * TILE)
    send(2 * TILE, TILE)
    for copy in copies:
        copy.wait()


def radial_stage(state, scale, mix, parts):
    vmem = pl.BlockSpec(memory_space=pltpu.VMEM)
    return pl.pallas_call(
        radial_body,
        out_shape=jax.ShapeDtypeStruct((parts, state.shape[0] // parts, state.shape[1]), jnp.float32),
        in_specs=[vmem] * 4,
        out_specs=pl.BlockSpec(memory_space=pltpu.HBM),
        scratch_shapes=[pltpu.VMEM(state.shape, jnp.float32), pltpu.SemaphoreType.DMA((6,))],
        name="radial_stage",
    )(*in_vmem(state, scale, *mix))


def last_body(state_ref, field_ref, th_ref, tl_ref, z_ref, out_ref, start, buffer, start_sems, sems):
    table_t = (th_ref[...], tl_ref[...])
    table_z = z_ref[...]
    pairs = start.shape[0] // 2
    rows = 12 * start.shape[0]
    state_ref = state_ref.reshape(state_ref.shape[0] // rows, rows, state_ref.shape[1])
    loads, copies = [], []
    for pair in range(pairs):
        planes = pl.ds(2 * pair, 2)
        loads.append(pltpu.make_async_copy(field_ref.at[planes], start.at[planes], start_sems.at[pair]))
        loads[-1].start()
    for pair in range(pairs):
        planes = pl.ds(2 * pair, 2)
        first, second = filter_pair(*unpack_pair(state_ref.at[:, pl.ds(24 * pair, 24), :]), table_t, table_z)
        loads[pair].wait()
        buffer[2 * pair] = first - start[2 * pair]
        buffer[2 * pair + 1] = second - start[2 * pair + 1]
        copies.append(pltpu.make_async_copy(buffer.at[planes], out_ref.at[planes], sems.at[pair]))
        copies[-1].start()
    for copy in copies:
        copy.wait()


def in_vmem(*arrays):
    return [pltpu.with_memory_space_constraint(array, pltpu.VMEM) for array in arrays]


def last_stage(state, field, table_t, table_z):
    vmem = pl.BlockSpec(memory_space=pltpu.VMEM)
    whole = pl.BlockSpec(memory_space=pl.ANY)
    (state,) = in_vmem(state)
    return pl.pallas_call(
        last_body,
        out_shape=jax.ShapeDtypeStruct(field.shape, jnp.float32),
        in_specs=[vmem, whole, vmem, vmem, vmem],
        out_specs=whole,
        scratch_shapes=[
            pltpu.VMEM(field.shape, jnp.float32),
            pltpu.VMEM(field.shape, jnp.float32),
            pltpu.SemaphoreType.DMA((field.shape[0] // 2,)),
            pltpu.SemaphoreType.DMA((field.shape[0] // 2,)),
        ],
        name="last_stage",
    )(state, field, *in_vmem(*table_t, table_z))


def swap(packed):
    return lax.all_to_all(packed, "space", 0, 0, tiled=True)


def shards(field, base, radial_step, az_shift, ax_shift, first_segment):
    state = field[0]
    count_t, count_z = state.shape[1:]
    parts = lax.axis_size("space")
    segment = lax.axis_index("seg")
    table_t = filter_table(count_t)
    table_z = filter_table(count_z)

    late = (STAGGER * ((segment + 1) // 2 % 2)).astype(jnp.int32)[None]
    with jax.named_scope("pack_base"):
        base_packed = pack_stage(base[0], parts, late)
    with jax.named_scope("base_to_points"):
        base_points = swap(base_packed)
    with jax.named_scope("first_filter"):
        high, low = split_constant(table_z)
        wide_z = np.block([[high, low], [high, np.zeros_like(low)]])
        rows = np.arange(count_t // 2)
        half_t = split_constant(halves(table_t)[np.concatenate([rows, count_t + rows])])
        filtered = first_stage(state, base[0], half_t, wide_z, parts)
    with jax.named_scope("shift_state"):
        filtered = from_behind(filtered, "seg", 1)
    with jax.named_scope("shift_base"):
        scale = coefficient_stage(base_points.reshape(-1, count_z), parts)
        scale = from_behind(scale, "seg", 1)
    with jax.named_scope("state_to_points"):
        points = swap(filtered)
    with jax.named_scope("radial"):
        points = radial_stage(points.reshape(-1, count_z), scale, mix_stage(radial_step, parts), parts)
    with jax.named_scope("state_to_radii"):
        carried = swap(points)

    with jax.named_scope("closing_tables"):
        closing = segment == first_segment[0] % lax.axis_size("seg")
        places_t = jnp.arange(count_t, dtype=jnp.int32)
        places_z = jnp.arange(count_z, dtype=jnp.int32)
        places_t = places_t[: count_t // 2]
        index_t = jnp.where(closing, (az_shift[0] - places_t) % count_t, places_t)
        index_t = jnp.concatenate([index_t, count_t + index_t])
        index_z = jnp.where(closing, (places_z + ax_shift[0]) % count_z, places_z)
        last_t = split_array(jnp.take(jnp.asarray(halves(table_t).astype(np.float32)), index_t, axis=0))
        last_z = jnp.take(jnp.asarray(table_z.astype(np.float32)), index_z, axis=0).T
        last_z = wide(*split_array(last_z))
    with jax.named_scope("last_filter"):
        return last_stage(carried.reshape(-1, count_z), state, last_t, last_z)[None]


def solution(mesh):
    in_specs = (P("seg", "space", None, None), P("seg", "space", None, None), P(), P(), P(), P())
    out_specs = P("seg", "space", None, None)
    return jax.shard_map(shards, mesh=mesh, in_specs=in_specs, out_specs=out_specs, check_vma=False)
```

```python
import math

import jax
import jax.numpy as jnp
import ml_dtypes
import numpy as np
from jax import lax
from jax.experimental import pallas as pl
from jax.experimental.pallas import tpu as pltpu
from jax.sharding import PartitionSpec as P

STEP_SIZE = 0.25
VISCOUS_RATE = 1.5e-05
STAGGER = 24000
TILE = 8


def filter_table(size):
    rows = np.arange(size)
    wave = np.where(rows == 0, 0, np.where(rows == 1, size // 2, rows // 2))
    angle = (wave[:, None] * rows[None, :] % size) * (2.0 * math.pi / size)
    sine = (rows % 2 == 1) & (rows >= 3)
    scale = np.where(rows < 2, math.sqrt(1.0 / size), math.sqrt(2.0 / size))
    table = scale[:, None] * np.where(sine[:, None], np.sin(angle), np.cos(angle))
    decay = np.exp(-VISCOUS_RATE * wave.astype(np.float64) ** 2)
    return table.T @ (decay[:, None] * table)


def halves(table):
    half = table.shape[0] // 2
    return np.concatenate([table[:, :half] + table[:, half:], table[:, :half] - table[:, half:]], 0) / 2


def split_constant(table):
    table = table.astype(np.float32)
    high = table.astype(ml_dtypes.bfloat16)
    return high, (table - high.astype(np.float32)).astype(ml_dtypes.bfloat16)


def split_array(array):
    high = lax.reduce_precision(array, 8, 7)
    return high.astype(jnp.bfloat16), (array - high).astype(jnp.bfloat16)


def split(value):
    high = value.astype(jnp.bfloat16)
    return high, (value - high.astype(jnp.float32)).astype(jnp.bfloat16)


def product(left, right):
    (left_high, left_low), (right_high, right_low) = left, right

    def dot(a, b):
        return jnp.dot(a, b, preferred_element_type=jnp.float32)

    return dot(left_high, right_high) + (dot(left_high, right_low) + dot(left_low, right_high))


def wide(high, low):
    return jnp.concatenate([jnp.concatenate([high, low], 1), jnp.concatenate([high, jnp.zeros_like(low)], 1)], 0)


def from_behind(block, axis, distance):
    devices = range(lax.axis_size(axis))
    route = [((i - distance) % len(devices), i) for i in devices]
    return lax.ppermute(block, axis, route)


def pack_pair(out_ref, first, second):
    parts = out_ref.shape[0]
    whole = parts * TILE
    count_z = first.shape[1]
    out_ref[:, 0:8, :] = first[:whole].reshape(parts, TILE, count_z)
    out_ref[:, 8:16, :] = second[:whole].reshape(parts, TILE, count_z)
    first = first[whole:].reshape(parts // 2, TILE, count_z)
    second = second[whole:].reshape(parts // 2, TILE, count_z)
    lower = lax.broadcasted_iota(jnp.int32, first.shape, 1) < TILE // 2
    even = jnp.where(lower, first, pltpu.roll(second, TILE // 2, 1))
    odd = jnp.where(lower, pltpu.roll(first, TILE // 2, 1), second)
    for k in range(parts // 2):
        out_ref[2 * k, 16:24, :] = even[k]
        out_ref[2 * k + 1, 16:24, :] = odd[k]


def unpack_pair(ref):
    parts, _, count_z = ref.shape
    whole = parts * TILE
    first = ref[:, 0:8, :].reshape(whole, count_z)
    second = ref[:, 8:16, :].reshape(whole, count_z)
    even = jnp.stack([ref[2 * k, 16:24, :] for k in range(parts // 2)])
    odd = jnp.stack([ref[2 * k + 1, 16:24, :] for k in range(parts // 2)])
    lower = lax.broadcasted_iota(jnp.int32, even.shape, 1) < TILE // 2
    first_rest = jnp.where(lower, even, pltpu.roll(odd, TILE // 2, 1)).reshape(whole // 2, count_z)
    second_rest = jnp.where(lower, pltpu.roll(even, TILE // 2, 1), odd).reshape(whole // 2, count_z)
    return jnp.concatenate([first, first_rest], 0), jnp.concatenate([second, second_rest], 0)


def filter_pair(first, second, table_t, table_z):
    count_z = first.shape[1]
    half = first.shape[0] // 2
    both = []
    for plane in (first, second):
        plane = jnp.dot(jnp.concatenate(split(plane), 1), table_z, preferred_element_type=jnp.float32)
        both.append(plane[:, :count_z] + plane[:, count_z:])
    both = jnp.concatenate(both, 1)
    even = product([table[:half] for table in table_t], split(both[:half] + both[half:]))
    odd = product([table[half:] for table in table_t], split(both[:half] - both[half:]))
    both = jnp.concatenate([even + odd, even - odd], 0)
    return both[:, :count_z], both[:, count_z:]


def pack_body(late_ref, base_ref, out_ref, start, packed, start_sems, sems):
    loads, copies = [], []
    for pair in range(start.shape[0] // 2):
        planes = pl.ds(2 * pair, 2)
        loads.append(pltpu.make_async_copy(base_ref.at[planes], start.at[planes], start_sems.at[pair]))
        loads[-1].start()
    for pair, load in enumerate(loads):
        rows = pl.ds(24 * pair, 24)
        load.wait()
        pack_pair(packed.at[:, rows, :], start[2 * pair], start[2 * pair + 1])
        copies.append(pltpu.make_async_copy(packed.at[:, rows, :], out_ref.at[:, rows, :], sems.at[pair]))
        copies[-1].start()
    pl.delay(late_ref[0])
    for copy in copies:
        copy.wait()


def pack_stage(base, parts, late):
    radii, count_t, count_z = base.shape
    shape = (parts, 12 * radii, count_z)
    hbm = pl.BlockSpec(memory_space=pltpu.HBM)
    return pl.pallas_call(
        pack_body,
        out_shape=jax.ShapeDtypeStruct(shape, jnp.float32),
        in_specs=[pl.BlockSpec(memory_space=pltpu.SMEM), hbm],
        out_specs=hbm,
        scratch_shapes=[
            pltpu.VMEM(base.shape, jnp.float32),
            pltpu.VMEM(shape, jnp.float32),
            pltpu.SemaphoreType.DMA((radii // 2,)),
            pltpu.SemaphoreType.DMA((radii // 2,)),
        ],
        name="pack_stage",
    )(late, base)


def first_body(field_ref, base_ref, th_ref, tl_ref, z_ref, state_ref):
    forced = [field_ref[k] + STEP_SIZE * base_ref[k] * field_ref[k] for k in range(2)]
    table_t = (th_ref[...], tl_ref[...])
    table_z = z_ref[...]
    pack_pair(state_ref, *filter_pair(*forced, table_t, table_z))


def first_stage(field, base, table_t, table_z, parts):
    radii, count_t, count_z = field.shape
    plane = pl.BlockSpec((2, count_t, count_z), lambda p: (p, 0, 0))
    whole_t = pl.BlockSpec((count_t, count_t // 2), lambda p: (0, 0))
    whole_z = pl.BlockSpec((2 * count_z, 2 * count_z), lambda p: (0, 0))
    return pl.pallas_call(
        first_body,
        out_shape=jax.ShapeDtypeStruct((parts, 12 * radii, count_z), jnp.float32),
        grid=(radii // 2,),
        in_specs=[plane, plane, whole_t, whole_t, whole_z],
        out_specs=pl.BlockSpec((parts, 24, count_z), lambda p: (0, p, 0)),
        name="first_stage",
    )(field, base, *table_t, table_z)


def row_of(pair, half, point):
    return 24 * pair + (TILE * half + point if point < TILE else 2 * TILE + 4 * half + point - TILE)


def load_points(ref, point, parts):
    stride = ref.shape[0] // parts
    rows = [ref[pl.ds(row_of(p, e, point), parts, stride), :] for p in range(3) for e in range(2)]
    return jnp.concatenate(rows, 0)


def coefficient_body(base_ref, out_ref):
    parts = out_ref.shape[1] // 6
    for point in range(out_ref.shape[0]):
        out_ref[point] = 1.0 + STEP_SIZE * load_points(base_ref, point, parts)


def coefficient_stage(base, parts):
    rows, count_z = base.shape
    vmem = pl.BlockSpec(memory_space=pltpu.VMEM)
    return pl.pallas_call(
        coefficient_body,
        out_shape=jax.ShapeDtypeStruct((12, rows // 12, count_z), jnp.float32),
        in_specs=[vmem],
        out_specs=vmem,
        name="coefficient_stage",
    )(base)


def mix_body(mix_ref, order_ref, high_ref, low_ref):
    order = order_ref[...]
    for part, out_ref in zip(split(mix_ref[...]), (high_ref, low_ref)):
        part = lax.dot_general(order, part, (((1,), (0,)), ((), ())), preferred_element_type=jnp.float32)
        part = part.astype(jnp.bfloat16)
        part = lax.dot_general(part, order, (((1,), (1,)), ((), ())), preferred_element_type=jnp.float32)
        out_ref[...] = part.astype(jnp.bfloat16)


def mix_stage(mix, parts):
    size = mix.shape[0]
    order = np.eye(size)[np.arange(size).reshape(parts, -1).T.reshape(-1)].astype(ml_dtypes.bfloat16)
    vmem = pl.BlockSpec(memory_space=pltpu.VMEM)
    shape = pltpu.VMEM(mix.shape, jnp.bfloat16)
    return pl.pallas_call(
        mix_body,
        out_shape=(shape, shape),
        in_specs=[vmem] * 2,
        out_specs=(vmem, vmem),
        name="mix_stage",
    )(mix, order)


def radial_body(state_ref, scale_ref, high_ref, low_ref, out_ref):
    parts = scale_ref.shape[1] // 6
    count_z = scale_ref.shape[2]
    stride = out_ref.shape[0] // parts
    mix = (high_ref[...], low_ref[...])
    for point in range(0, scale_ref.shape[0], 2):
        state = jnp.concatenate([load_points(state_ref, point + k, parts) for k in range(2)], 1)
        scale = jnp.concatenate([scale_ref[point + k] for k in range(2)], 1)
        state = product(mix, split(state)) * scale
        state = product(mix, split(state))
        for k in range(2):
            for p in range(3):
                for e in range(2):
                    radius = (2 * p + e) * parts
                    out_ref[pl.ds(row_of(p, e, point + k), parts, stride), :] = state[
                        radius : radius + parts, k * count_z : (k + 1) * count_z
                    ]


def radial_stage(state, scale, mix):
    vmem = pl.BlockSpec(memory_space=pltpu.VMEM)
    return pl.pallas_call(
        radial_body,
        out_shape=jax.ShapeDtypeStruct(state.shape, jnp.float32),
        in_specs=[vmem] * 4,
        out_specs=vmem,
        name="radial_stage",
    )(*in_vmem(state, scale, *mix))


def last_body(state_ref, field_ref, th_ref, tl_ref, z_ref, out_ref, start, buffer, start_sems, sems):
    table_t = (th_ref[...], tl_ref[...])
    table_z = z_ref[...]
    pairs = start.shape[0] // 2
    rows = 12 * start.shape[0]
    state_ref = state_ref.reshape(state_ref.shape[0] // rows, rows, state_ref.shape[1])
    loads, copies = [], []
    for pair in range(pairs):
        planes = pl.ds(2 * pair, 2)
        loads.append(pltpu.make_async_copy(field_ref.at[planes], start.at[planes], start_sems.at[pair]))
        loads[-1].start()
    for pair in range(pairs):
        planes = pl.ds(2 * pair, 2)
        first, second = filter_pair(*unpack_pair(state_ref.at[:, pl.ds(24 * pair, 24), :]), table_t, table_z)
        loads[pair].wait()
        buffer[2 * pair] = first - start[2 * pair]
        buffer[2 * pair + 1] = second - start[2 * pair + 1]
        copies.append(pltpu.make_async_copy(buffer.at[planes], out_ref.at[planes], sems.at[pair]))
        copies[-1].start()
    for copy in copies:
        copy.wait()


def in_vmem(*arrays):
    return [pltpu.with_memory_space_constraint(array, pltpu.VMEM) for array in arrays]


def last_stage(state, field, table_t, table_z):
    vmem = pl.BlockSpec(memory_space=pltpu.VMEM)
    whole = pl.BlockSpec(memory_space=pl.ANY)
    (state,) = in_vmem(state)
    return pl.pallas_call(
        last_body,
        out_shape=jax.ShapeDtypeStruct(field.shape, jnp.float32),
        in_specs=[vmem, whole, vmem, vmem, vmem],
        out_specs=whole,
        scratch_shapes=[
            pltpu.VMEM(field.shape, jnp.float32),
            pltpu.VMEM(field.shape, jnp.float32),
            pltpu.SemaphoreType.DMA((field.shape[0] // 2,)),
            pltpu.SemaphoreType.DMA((field.shape[0] // 2,)),
        ],
        name="last_stage",
    )(state, field, *in_vmem(*table_t, table_z))


def swap(packed):
    return lax.all_to_all(packed, "space", 0, 0, tiled=True)


def shards(field, base, radial_step, az_shift, ax_shift, first_segment):
    state = field[0]
    count_t, count_z = state.shape[1:]
    parts = lax.axis_size("space")
    segment = lax.axis_index("seg")
    table_t = filter_table(count_t)
    table_z = filter_table(count_z)

    late = (STAGGER * ((segment + 1) // 2 % 2)).astype(jnp.int32)[None]
    with jax.named_scope("pack_base"):
        base_packed = pack_stage(base[0], parts, late)
    with jax.named_scope("base_to_points"):
        base_points = swap(base_packed)
    with jax.named_scope("first_filter"):
        high, low = split_constant(table_z)
        wide_z = np.block([[high, low], [high, np.zeros_like(low)]])
        rows = np.arange(count_t // 2)
        half_t = split_constant(halves(table_t)[np.concatenate([rows, count_t + rows])])
        filtered = first_stage(state, base[0], half_t, wide_z, parts)
    with jax.named_scope("shift_state"):
        filtered = from_behind(filtered, "seg", 1)
    with jax.named_scope("shift_base"):
        scale = coefficient_stage(base_points.reshape(-1, count_z), parts)
        scale = from_behind(scale, "seg", 1)
    with jax.named_scope("state_to_points"):
        points = swap(filtered)
    with jax.named_scope("radial"):
        points = radial_stage(points.reshape(-1, count_z), scale, mix_stage(radial_step, parts))
    with jax.named_scope("state_to_radii"):
        carried = swap(points.reshape(parts, -1, count_z))

    with jax.named_scope("closing_tables"):
        closing = segment == first_segment[0] % lax.axis_size("seg")
        places_t = jnp.arange(count_t, dtype=jnp.int32)
        places_z = jnp.arange(count_z, dtype=jnp.int32)
        places_t = places_t[: count_t // 2]
        index_t = jnp.where(closing, (az_shift[0] - places_t) % count_t, places_t)
        index_t = jnp.concatenate([index_t, count_t + index_t])
        index_z = jnp.where(closing, (places_z + ax_shift[0]) % count_z, places_z)
        last_t = split_array(jnp.take(jnp.asarray(halves(table_t).astype(np.float32)), index_t, axis=0))
        last_z = jnp.take(jnp.asarray(table_z.astype(np.float32)), index_z, axis=0).T
        last_z = wide(*split_array(last_z))
    with jax.named_scope("last_filter"):
        return last_stage(carried.reshape(-1, count_z), state, last_t, last_z)[None]


def solution(mesh):
    in_specs = (P("seg", "space", None, None), P("seg", "space", None, None), P(), P(), P(), P())
    out_specs = P("seg", "space", None, None)
    return jax.shard_map(shards, mesh=mesh, in_specs=in_specs, out_specs=out_specs, check_vma=False)
```
